128 devices in a mesh: ctx: 32 (over y, z_lo, x), page: 4 (over z_hi, core).
Axes of the slice: x: 4, y: 4, z: 4 (z_hi: 2, z_lo: 2; z = z_hi * 2 + z_lo), core: 2. Of those that a mesh axis runs over, the one named last changes fastest.
Arguments:
- queries: bfloat16 [8192, 8192], P('ctx', 'page'), may hold values from -200 to 200
- keys: bfloat16 [8192, 512], P('ctx', 'page'), may hold values from -6 to 6
- values: bfloat16 [8192, 512], P('ctx', 'page'), may hold values from -6 to 6
- span_table: int32 [64], replicated, may hold values from 0 to 63, each once
- page_slots: int32 [64], replicated, may hold values from 0 to 63, each once
Outputs:
- attended: bfloat16 [8192, 8192], P('ctx', 'page')
- cache_pages: bfloat16 [64, 4, 2, 128, 128], P('ctx')
- cache_scales: float32 [64, 4, 2], P('ctx')
The draws below stay inside these ranges and needn't reach their ends.
Inputs may be any that keep to these rules, and one draw needn't show every extreme that they name: Stored span i (rows i * 128 to (i + 1) * 128 - 1) holds prompt positions span_table[i] * 128 onward; every value appears once. `page_slots`: every slot is named by exactly one page.
All inputs are finite; a program needn't handle non-finite values. Where the reference program divides by a largest or mean magnitude, that divisor is 1e-20 or more.
Results may differ from the reference program's by a relative error of at most 0.0055.
Values may be sent and summed in bfloat16 or wider, within the bound.
No kernel may reach another device: no remote copies, remote signals or barrier semaphores. Data moves between devices by JAX's collectives and lax.ppermute only.
A program may use at most 64 MiB of HBM per device.

```python
import jax
import jax.numpy as jnp
from jax import lax

HQ = 64
KVH = 4
DH = 128
PAGE = 128
SPAN = 128
TOKENS = 8192
SLOTS = 64
N_CTX = 32


def common_draw(key):
    key_rows = jax.random.truncated_normal(jax.random.fold_in(key, 11), -6.0, 6.0, (TOKENS, KVH * DH), jnp.float32)
    query_rows = jax.random.truncated_normal(jax.random.fold_in(key, 12), -6.0, 6.0, (TOKENS, HQ * DH), jnp.float32)
    return (query_rows, key_rows)


def draw_queries(key, part):
    return common_draw(key)[0].astype(jnp.bfloat16)


def draw_keys(key, part):
    return common_draw(key)[1].astype(jnp.bfloat16)


def level_of(stream_key, shape, pieces, smallest, high):
    gain, own = 1.0, jax.random.fold_in(stream_key, 6)
    for dim, blocks in pieces:
        draws = jnp.exp(jax.random.uniform(jax.random.fold_in(own, dim), (blocks,), jnp.float32, smallest / len(pieces), high / len(pieces)))
        gain = gain * jnp.repeat(draws, shape[dim] // blocks).reshape([-1 if axis == dim else 1 for axis in range(len(shape))])
    return gain


def gaussian(rng, shape, scale, limit, shards=(), kind=jnp.bfloat16):
    level = level_of(rng, shape, shards, -0.22, 0.18) if shards else 1.0
    values = jax.random.normal(rng, shape, jnp.float32) * scale * level
    return jnp.minimum(jnp.maximum(values, -limit), limit).astype(kind)


def setup_inputs(seed: int = 0) -> dict:
    splits = jax.random.split(jax.random.key(seed), 6)
    return {
        "queries": draw_queries(jax.random.fold_in(splits[5], 71), 0),
        "keys": draw_keys(jax.random.fold_in(splits[5], 71), 0),
        "values": gaussian(splits[2], (TOKENS, KVH * DH), 1.0, 6.0, ((0, 32), (1, 4))),
        "span_table": jax.random.permutation(splits[3], 2 * N_CTX).astype(jnp.int32),
        "page_slots": jax.random.permutation(splits[4], SLOTS).astype(jnp.int32),
    }


def reference(queries, keys, values, span_table, page_slots):
    rows = jnp.arange(TOKENS, dtype=jnp.int32)
    pos = span_table[rows // SPAN] * SPAN + rows % SPAN
    group = HQ // KVH
    key_heads = keys.reshape(TOKENS, KVH, DH).astype(jnp.float32)
    value_heads = values.reshape(TOKENS, KVH, DH).astype(jnp.float32)
    scale = DH ** -0.5

    def block(index):
        start = (index * SPAN).astype(jnp.int32)
        query_block = lax.dynamic_slice_in_dim(queries, start, SPAN, 0)
        query_block = query_block.reshape(SPAN, KVH, group, DH).astype(jnp.float32)
        query_pos = lax.dynamic_slice_in_dim(pos, start, SPAN, 0)
        score = jnp.einsum('qhgd,khd->hgqk', query_block, key_heads) * scale
        keep = pos[None, :] <= query_pos[:, None]
        score = jnp.where(keep[None, None], score, -1e30)
        top = jnp.max(score, axis=-1, keepdims=True)
        weight = jnp.where(keep[None, None], jnp.exp(score - top), 0.0)
        total = jnp.sum(weight, axis=-1)
        weight_b = weight.astype(jnp.bfloat16).astype(jnp.float32)
        summed = jnp.einsum('hgqk,khd->qhgd', weight_b, value_heads)
        result = summed / jnp.transpose(total, (2, 0, 1))[..., None]
        return result.reshape(SPAN, HQ * DH).astype(jnp.bfloat16)

    attended = lax.map(block, jnp.arange(TOKENS // SPAN, dtype=jnp.int32)).reshape(TOKENS, HQ * DH)
    key_pages = keys.reshape(SLOTS, PAGE, KVH, DH).transpose(0, 2, 1, 3)
    value_pages = values.reshape(SLOTS, PAGE, KVH, DH).transpose(0, 2, 1, 3)
    stacked = jnp.stack([key_pages, value_pages], axis=2)
    page_of_slot = jnp.zeros((SLOTS,), jnp.int32).at[page_slots].set(jnp.arange(SLOTS, dtype=jnp.int32))
    raw = stacked[page_of_slot].astype(jnp.float32)
    cache_scales = jnp.max(jnp.abs(raw), axis=(3, 4)) + 1e-6
    cache_pages = (raw / cache_scales[..., None, None]).astype(jnp.bfloat16)
    return attended, cache_pages, cache_scales
```

```python
import functools

import jax
import jax.numpy as jnp
from jax import lax
from jax.experimental import pallas as pl
from jax.experimental.pallas import tpu as pltpu
from jax.sharding import Mesh, PartitionSpec as P

DH = 128
SP = 128
HEADS = 16
ROWS = HEADS * SP
SCALE2 = DH ** (-0.5) * 1.4426950408889634
TILE = 512
GROUP = 8
LIMIT = 2.0**100
NT = (((1,), (1,)), ((), ()))
MASKS = ((1, 3), (3, 1))
VM = pl.BlockSpec(memory_space=pltpu.VMEM)
SM = pl.BlockSpec(memory_space=pltpu.SMEM)


def coords():
    return tuple(lax.axis_index(a) for a in ("y", "zl", "x", "core"))


def own_ctx():
    y, zl, x, _ = coords()
    return y * 8 + zl * 4 + x


def span_of(piece, part):
    y, zl, x, core = coords()
    a, b = MASKS[part]
    bit = lambda i: (piece >> i) & 1
    first = (bit(1) * a) ^ (bit(2) * b)
    second = (bit(3) * a) ^ (bit(4) * b)
    dx = jnp.where(core == 0, first, second)
    dy = jnp.where(core == 0, second, first)
    return ((y ^ dy) * 8 + (zl ^ bit(0)) * 4 + (x ^ dx)) * 2 + part


def fill(kbuf, vbuf, refs):
    ones = jnp.ones((SP, DH), jnp.bfloat16)
    at = 0
    for ref in refs:
        for i in range(ref.shape[0]):
            kbuf[at * SP : (at + 1) * SP, :] = ref[i, 0]
            vbuf[at * SP : (at + 1) * SP, :DH] = ref[i, 1]
            vbuf[at * SP : (at + 1) * SP, DH:] = ones
            at += 1
    kbuf[at * SP : (at + 1) * SP, :] = jnp.zeros((SP, DH), jnp.bfloat16)
    vbuf[at * SP : (at + 1) * SP, :] = jnp.zeros((SP, 2 * DH), jnp.bfloat16)


def listed(lst, table, limit, per_part, first, total):
    def add(i, n):
        for part in range(2):
            lst[n] = i + part * per_part
            n = n + (table[span_of(first + i, part)] < limit).astype(jnp.int32)
        return n

    n = lax.fori_loop(0, per_part, add, 0)
    for i in range(GROUP):
        lst[n + i] = total
    return n


def group_blocks(lst, kbuf, vbuf, j):
    ks, vs = [], []
    for i in range(GROUP):
        at = pl.multiple_of(lst[j * GROUP + i] * SP, SP)
        ks.append(kbuf[pl.ds(at, SP), :])
        vs.append(vbuf[pl.ds(at, SP), :])
    return jnp.concatenate(ks, 0), jnp.concatenate(vs, 0)


def tile_update(q, kg, vg, top):
    score = lax.dot_general(q, kg, NT, preferred_element_type=jnp.float32)
    weight = jnp.exp2(score * SCALE2 - jnp.concatenate([top] * GROUP, axis=1))
    return jnp.dot(weight.astype(jnp.bfloat16), vg, preferred_element_type=jnp.float32)


def run_groups(s, n, start, q_ref, top_ref, acc, lst, kbuf, vbuf):
    def group(j, carry):
        kg, vg = group_blocks(lst, kbuf, vbuf, j)
        for r in range(0, ROWS, TILE):
            at = slice(r, r + TILE)
            acc[s, at, :] += tile_update(q_ref[s, at, :], kg, vg, top_ref[s, at, :])
        return carry

    lax.fori_loop(start, (n + GROUP - 1) // GROUP, group, 0)


def first_kernel(table, q_ref, a_ref, b_ref, qs, top_ref, acc, kbuf, vbuf, lst):
    per_part = a_ref.shape[0]
    fill(kbuf, vbuf, (a_ref, b_ref))
    for s in range(2):
        for h in range(HEADS):
            qs[s, h * SP : (h + 1) * SP, :] = q_ref[s * SP : (s + 1) * SP, h * DH : (h + 1) * DH]
    for s in range(2):
        own = s * per_part * SP
        key = kbuf[own : own + SP, :]
        value = vbuf[own : own + SP, :]
        for r in range(0, ROWS, TILE):
            at = slice(r, r + TILE)
            score = lax.dot_general(qs[s, at, :], key, NT, preferred_element_type=jnp.float32)
            row = lax.broadcasted_iota(jnp.int32, (TILE, SP), 0) % SP
            keep = lax.broadcasted_iota(jnp.int32, (TILE, SP), 1) <= row
            score = jnp.where(keep, score * SCALE2, -1e30)
            top = jnp.broadcast_to(jnp.max(score, axis=1, keepdims=True), (TILE, SP))
            top_ref[s, at, :] = top
            weight = jnp.where(keep, jnp.exp2(score - top), 0.0).astype(jnp.bfloat16)
            acc[s, at, :] = jnp.dot(weight, value, preferred_element_type=jnp.float32)
        limit = table[own_ctx() * 2 + s]
        n = listed(lst, table, limit, per_part, 0, 2 * per_part)
        run_groups(s, n, 0, qs, top_ref, acc, lst, kbuf, vbuf)


def next_kernel(table, qs, top_ref, a_ref, b_ref, acc, kbuf, vbuf, lst):
    per_part = a_ref.shape[0]
    fill(kbuf, vbuf, (a_ref, b_ref))
    for s in range(2):
        limit = table[own_ctx() * 2 + s]
        n = listed(lst, table, limit, per_part, per_part, 2 * per_part)
        kg, vg = group_blocks(lst, kbuf, vbuf, 0)
        for r in range(0, ROWS, TILE):
            at = slice(r, r + TILE)
            acc[s, at, :] = tile_update(qs[s, at, :], kg, vg, top_ref[s, at, :])
        run_groups(s, n, 1, qs, top_ref, acc, lst, kbuf, vbuf)


def last_kernel(
    table, qs, top_ref, acc1, acc2, sa, sb, a_ref, b_ref, out, acc, worst, kbuf, vbuf, lst, hold
):
    next_kernel(table, qs, top_ref, a_ref, b_ref, acc, kbuf, vbuf, lst)
    worst[...] = jnp.zeros_like(worst)
    for s in range(2):
        for h in range(HEADS):
            at = slice(h * SP, (h + 1) * SP)
            both = acc[s, at, :] + (acc1[s, at, :] + acc2[s, at, :])
            total = both[:, DH:]
            worst[...] = jnp.where(total < LIMIT, worst[...], 1.0)
            out[s * SP : (s + 1) * SP, h * DH : (h + 1) * DH] = (both[:, :DH] / total).astype(
                jnp.bfloat16
            )

    @pl.when(jnp.max(worst[...]) > 0.0)
    def _():
        rescaled(table, qs, sa, sb, a_ref, b_ref, out, acc, hold)


def rescaled(table, qs, sa, sb, a_ref, b_ref, out, acc, hold):
    for s in range(2):
        limit = table[own_ctx() * 2 + s]
        hold[...] = jnp.full_like(hold, -1e30)
        acc[s] = jnp.zeros_like(acc[s])
        for part, refs in ((0, (sa, a_ref)), (1, (sb, b_ref))):
            for half, ref in enumerate(refs):

                def block(i, carry, ref=ref, part=part, half=half):
                    pos = table[span_of(half * ref.shape[0] + i, part)]

                    @pl.when(pos <= limit)
                    def _():
                        key = ref[i, 0]
                        value = ref[i, 1]

                        def head(h, c):
                            at = pl.ds(pl.multiple_of(h * SP, SP), SP)
                            score = lax.dot_general(
                                qs[s, at, :], key, NT, preferred_element_type=jnp.float32
                            )
                            row = lax.broadcasted_iota(jnp.int32, (SP, SP), 0)
                            col = lax.broadcasted_iota(jnp.int32, (SP, SP), 1)
                            keep = (col + pos * SP) <= (row + limit * SP)
                            score = jnp.where(keep, score * SCALE2, -1e30)
                            old = hold[at, :]
                            new = jnp.maximum(old, jnp.max(score, axis=1, keepdims=True))
                            hold[at, :] = new
                            factor = jnp.exp2(old - new)
                            weight = jnp.where(keep, jnp.exp2(score - new), 0.0)
                            acc[s, at, :DH] = acc[s, at, :DH] * factor + jnp.dot(
                                weight.astype(jnp.bfloat16),
                                value,
                                preferred_element_type=jnp.float32,
                            )
                            acc[s, at, DH:] = acc[s, at, DH:] * factor + jnp.sum(
                                weight, axis=1, keepdims=True
                            )
                            return c

                        lax.fori_loop(0, HEADS, head, 0)

                    return carry

                lax.fori_loop(0, ref.shape[0], block, 0)
        for h in range(HEADS):
            at = slice(h * SP, (h + 1) * SP)
            out[s * SP : (s + 1) * SP, h * DH : (h + 1) * DH] = (
                acc[s, at, :DH] / acc[s, at, DH:]
            ).astype(jnp.bfloat16)


def page_kernel(slots, sa, sb, a_ref, b_ref, pages, scales):
    for part, refs in ((0, (sa, a_ref)), (1, (sb, b_ref))):
        for half, ref in enumerate(refs):

            def block(i, carry, ref=ref, part=part, half=half):
                slot = slots[span_of(half * ref.shape[0] + i, part)]

                @pl.when(slot // 2 == own_ctx())
                def _():
                    j = slot % 2
                    for kind in range(2):
                        raw = ref[i, kind].astype(jnp.float32)
                        high = jnp.max(jnp.abs(raw), axis=0, keepdims=True)
                        scale = jnp.max(high, axis=1, keepdims=True) + 1e-06
                        pages[j, kind] = (raw / scale).astype(jnp.bfloat16)
                        scales[j, pl.ds(kind, 1), :] = jnp.broadcast_to(scale, (1, DH))

                return carry

            lax.fori_loop(0, ref.shape[0], block, 0)


def params():
    return pltpu.CompilerParams(vmem_limit_bytes=56 * 2**20)


def f32(*shape):
    return jax.ShapeDtypeStruct(shape, jnp.float32)


def bf16(*shape):
    return jax.ShapeDtypeStruct(shape, jnp.bfloat16)


def cost(spans):
    return pl.CostEstimate(
        flops=4 * 2 * ROWS * spans * SP * DH * 2,
        transcendentals=2 * ROWS * spans * SP,
        bytes_accessed=8 * 2**20,
    )


def buffers(blocks):
    return [
        pltpu.VMEM(((blocks + 1) * SP, DH), jnp.bfloat16),
        pltpu.VMEM(((blocks + 1) * SP, 2 * DH), jnp.bfloat16),
        pltpu.SMEM((blocks + 2 * GROUP,), jnp.int32),
    ]


def swap(x, along_first, mask):
    pairs = []
    for y in range(4):
        for xx in range(4):
            for core in range(2):
                on_x = (core == 0) == along_first
                there = (y, xx ^ mask) if on_x else (y ^ mask, xx)
                pairs.append(((y * 4 + xx) * 2 + core, (there[0] * 4 + there[1]) * 2 + core))
    return lax.ppermute(x, ("y", "x", "core"), pairs)


def on_device(queries, keys, values, span_table, page_slots):
    own = jnp.stack([keys.reshape(2, SP, DH), values.reshape(2, SP, DH)], axis=1)[:, None]
    both = jnp.concatenate([own, lax.ppermute(own, "zl", [(0, 1), (1, 0)])], axis=1)
    held = [both[0], both[1]]
    for stage in range(2):
        come = [swap(held[p], True, MASKS[p][stage]) for p in range(2)]
        held = [jnp.concatenate([held[p], come[p]], axis=0) for p in range(2)]
    come = [swap(held[p], False, MASKS[p][0]) for p in range(2)]
    state = f32(2, ROWS, 2 * DH)
    qs, top, acc1 = pl.pallas_call(
        first_kernel,
        out_shape=(bf16(2, ROWS, DH), f32(2, ROWS, DH), state),
        in_specs=[SM] + [VM] * 3,
        out_specs=(VM, VM, VM),
        scratch_shapes=buffers(16),
        compiler_params=params(),
        cost_estimate=cost(16),
        name="attend_first",
    )(span_table, queries, held[0], held[1])
    more = come
    held = [jnp.concatenate([held[p], come[p]], axis=0) for p in range(2)]
    come = [swap(held[p], False, MASKS[p][1]) for p in range(2)]
    acc2 = pl.pallas_call(
        next_kernel,
        out_shape=state,
        in_specs=[SM] + [VM] * 4,
        out_specs=VM,
        scratch_shapes=buffers(16),
        compiler_params=params(),
        cost_estimate=cost(16),
        name="attend_next",
    )(span_table, qs, top, more[0], more[1])
    pages, scales = pl.pallas_call(
        page_kernel,
        out_shape=(bf16(2, 2, SP, DH), f32(2, 2, DH)),
        in_specs=[SM] + [VM] * 4,
        out_specs=(VM, VM),
        compiler_params=params(),
        name="pick_pages",
    )(page_slots, held[0], held[1], come[0], come[1])
    attended = pl.pallas_call(
        last_kernel,
        out_shape=bf16(2 * SP, HEADS * DH),
        in_specs=[SM] + [VM] * 8,
        out_specs=VM,
        scratch_shapes=[pltpu.VMEM((2, ROWS, 2 * DH), jnp.float32), pltpu.VMEM((SP, DH), jnp.float32)]
        + buffers(32)
        + [pltpu.VMEM((ROWS, DH), jnp.float32)],
        compiler_params=params(),
        cost_estimate=cost(32),
        name="attend_last",
    )(span_table, qs, top, acc1, acc2, held[0], held[1], come[0], come[1])
    all_pages = lax.all_gather(pages, ("zh", "core"), axis=0)
    all_scales = lax.all_gather(scales[:, :, 0], ("zh", "core"), axis=0)
    return attended, all_pages.transpose(1, 0, 2, 3, 4), all_scales.transpose(1, 0, 2)


def solution(mesh):
    fine = Mesh(mesh.devices.reshape(4, 2, 4, 2, 2), ("y", "zl", "x", "zh", "core"))
    ctx, page = ("y", "zl", "x"), ("zh", "core")
    return jax.shard_map(
        on_device,
        mesh=fine,
        in_specs=(P(ctx, page), P(ctx, page), P(ctx, page), P(), P()),
        out_specs=(P(ctx, page), P(ctx, None, None, None, None), P(ctx, None, None)),
        check_vma=False,
    )
```

```python
import functools

import jax
import jax.numpy as jnp
from jax import lax
from jax.experimental import pallas as pl
from jax.experimental.pallas import tpu as pltpu
from jax.sharding import Mesh, PartitionSpec as P

DH = 128
SP = 128
HEADS = 16
ROWS = HEADS * SP
SCALE2 = DH ** (-0.5) * 1.4426950408889634
TILE = 512
GROUP = 16
LIMIT = 2.0**100
NT = (((1,), (1,)), ((), ()))
MASKS = ((1, 3), (3, 1))
ANY = pl.BlockSpec(memory_space=pl.ANY)
VM = pl.BlockSpec(memory_space=pltpu.VMEM)
SM = pl.BlockSpec(memory_space=pltpu.SMEM)


def coords():
    return tuple(lax.axis_index(a) for a in ("y", "zl", "x", "core"))


def own_ctx():
    y, zl, x, _ = coords()
    return y * 8 + zl * 4 + x


def span_of(piece, part):
    y, zl, x, core = coords()
    a, b = MASKS[part]
    bit = lambda i: (piece >> i) & 1
    first = (bit(1) * a) ^ (bit(2) * b)
    second = (bit(3) * a) ^ (bit(4) * b)
    dx = jnp.where(core == 0, first, second)
    dy = jnp.where(core == 0, second, first)
    return ((y ^ dy) * 8 + (zl ^ bit(0)) * 4 + (x ^ dx)) * 2 + part


def fill(kbuf, vbuf, refs):
    ones = jnp.ones((SP, DH), jnp.bfloat16)
    at = 0
    for ref in refs:
        for i in range(ref.shape[0]):
            kbuf[at * SP : (at + 1) * SP, :] = ref[i, 0]
            vbuf[at * SP : (at + 1) * SP, :DH] = ref[i, 1]
            vbuf[at * SP : (at + 1) * SP, DH:] = ones
            at += 1
    kbuf[at * SP : (at + 1) * SP, :] = jnp.zeros((SP, DH), jnp.bfloat16)
    vbuf[at * SP : (at + 1) * SP, :] = jnp.zeros((SP, 2 * DH), jnp.bfloat16)


def stack_heads(qs, q_ref, s):
    for h in range(HEADS):
        qs[s, h * SP : (h + 1) * SP, :] = q_ref[s * SP : (s + 1) * SP, h * DH : (h + 1) * DH]


def listed(lst, table, limit, per_part, first, total):
    def add(i, n):
        for part in range(2):
            lst[n] = i + part * per_part
            n = n + (table[span_of(first + i, part)] < limit).astype(jnp.int32)
        return n

    n = lax.fori_loop(0, per_part, add, 0)
    for i in range(GROUP):
        lst[n + i] = total
    return n


def tiles_update(s, at, group, fresh, qs, top_ref, acc, lst, kbuf, vbuf):
    ks, vs = [], []
    for i in range(group):
        begin = pl.multiple_of(lst[at + i] * SP, SP)
        ks.append(kbuf[pl.ds(begin, SP), :])
        vs.append(vbuf[pl.ds(begin, SP), :])
    kg, vg = jnp.concatenate(ks, 0), jnp.concatenate(vs, 0)
    for r in range(0, ROWS, TILE):
        at = slice(r, r + TILE)
        score = lax.dot_general(qs[s, at, :], kg, NT, preferred_element_type=jnp.float32)
        top = jnp.concatenate([top_ref[s, at, :]] * group, axis=1)
        weight = jnp.exp2(score * SCALE2 - top).astype(jnp.bfloat16)
        update = jnp.dot(weight, vg, preferred_element_type=jnp.float32)
        acc[s, at, :] = update if fresh else acc[s, at, :] + update


def run_groups(s, n, start, *refs):
    whole = (n + GROUP // 2 - 1) // GROUP

    def group(j, carry):
        tiles_update(s, j * GROUP, GROUP, False, *refs)
        return carry

    lax.fori_loop(start, whole, group, 0)

    @pl.when(n > jnp.maximum(whole, start) * GROUP)
    def _():
        tiles_update(s, jnp.maximum(whole, start) * GROUP, GROUP // 2, False, *refs)


def first_kernel(table, q_ref, a_ref, b_ref, top_out, acc_out, qs, top_ref, acc, kbuf, vbuf, lst, sems):
    per_part = a_ref.shape[0]
    fill(kbuf, vbuf, (a_ref, b_ref))
    copies = []
    for s in range(2):
        stack_heads(qs, q_ref, s)
        own = s * per_part * SP
        key = kbuf[own : own + SP, :]
        value = vbuf[own : own + SP, :]
        for r in range(0, ROWS, TILE):
            at = slice(r, r + TILE)
            score = lax.dot_general(qs[s, at, :], key, NT, preferred_element_type=jnp.float32)
            row = lax.broadcasted_iota(jnp.int32, (TILE, SP), 0) % SP
            keep = lax.broadcasted_iota(jnp.int32, (TILE, SP), 1) <= row
            score = jnp.where(keep, score * SCALE2, -1e30)
            top = jnp.broadcast_to(jnp.max(score, axis=1, keepdims=True), (TILE, SP))
            top_ref[s, at, :] = top
            weight = jnp.where(keep, jnp.exp2(score - top), 0.0).astype(jnp.bfloat16)
            acc[s, at, :] = jnp.dot(weight, value, preferred_element_type=jnp.float32)
        copies.append(pltpu.make_async_copy(top_ref.at[s], top_out.at[s], sems.at[0, s]))
        copies[-1].start()
        limit = table[own_ctx() * 2 + s]
        n = listed(lst, table, limit, per_part, 0, 2 * per_part)
        run_groups(s, n, 0, qs, top_ref, acc, lst, kbuf, vbuf)
        copies.append(pltpu.make_async_copy(acc.at[s], acc_out.at[s], sems.at[1, s]))
        copies[-1].start()
    for copy in copies:
        copy.wait()


def next_span(s, table, q_ref, per_part, qs, top_ref, acc, kbuf, vbuf, lst):
    stack_heads(qs, q_ref, s)
    limit = table[own_ctx() * 2 + s]
    n = listed(lst, table, limit, per_part, per_part, 2 * per_part)
    tiles_update(s, 0, GROUP, True, qs, top_ref, acc, lst, kbuf, vbuf)
    run_groups(s, n, 1, qs, top_ref, acc, lst, kbuf, vbuf)


def next_kernel(
    table, q_ref, top_in, a_ref, b_ref, acc_out, qs, top_ref, acc, kbuf, vbuf, lst, sems
):
    tops = [pltpu.make_async_copy(top_in.at[s], top_ref.at[s], sems.at[0, s]) for s in range(2)]
    for copy in tops:
        copy.start()
    per_part = a_ref.shape[0]
    fill(kbuf, vbuf, (a_ref, b_ref))
    outs = []
    for s in range(2):
        tops[s].wait()
        next_span(s, table, q_ref, per_part, qs, top_ref, acc, kbuf, vbuf, lst)
        outs.append(pltpu.make_async_copy(acc.at[s], acc_out.at[s], sems.at[1, s]))
        outs[-1].start()
    for copy in outs:
        copy.wait()


def last_kernel(
    table, q_ref, top_in, acc1_in, acc2_in, a_ref, b_ref, sa, sb, out,
    qs, top_ref, acc, kbuf, vbuf, lst, sems, acc1, acc2, worst, hold, sa_v, sb_v, far,
):
    tops = [pltpu.make_async_copy(top_in.at[s], top_ref.at[s], sems.at[0, s]) for s in range(2)]
    ones = [pltpu.make_async_copy(acc1_in.at[s], acc1.at[s], sems.at[1, s]) for s in range(2)]
    twos = [pltpu.make_async_copy(acc2_in.at[s], acc2.at[s], sems.at[2, s]) for s in range(2)]
    for s in range(2):
        for copies in (tops, ones, twos):
            copies[s].start()
    per_part = a_ref.shape[0]
    fill(kbuf, vbuf, (a_ref, b_ref))
    worst[...] = jnp.zeros_like(worst)
    for s in range(2):
        tops[s].wait()
        next_span(s, table, q_ref, per_part, qs, top_ref, acc, kbuf, vbuf, lst)
        ones[s].wait()
        twos[s].wait()
        for h in range(HEADS):
            at = slice(h * SP, (h + 1) * SP)
            both = acc[s, at, :] + (acc1[s, at, :] + acc2[s, at, :])
            total = both[:, DH:]
            worst[...] = jnp.where(total < LIMIT, worst[...], 1.0)
            out[s * SP : (s + 1) * SP, h * DH : (h + 1) * DH] = (both[:, :DH] / total).astype(
                jnp.bfloat16
            )

    @pl.when(jnp.max(worst[...]) > 0.0)
    def _():
        fetch = [
            pltpu.make_async_copy(sa, sa_v, far.at[0]),
            pltpu.make_async_copy(sb, sb_v, far.at[1]),
        ]
        for copy in fetch:
            copy.start()
        for copy in fetch:
            copy.wait()
        rescaled(table, qs, sa_v, sb_v, a_ref, b_ref, out, acc, hold)


def rescaled(table, qs, sa, sb, a_ref, b_ref, out, acc, hold):
    for s in range(2):
        limit = table[own_ctx() * 2 + s]
        hold[...] = jnp.full_like(hold, -1e30)
        acc[s] = jnp.zeros_like(acc[s])
        for part, refs in ((0, (sa, a_ref)), (1, (sb, b_ref))):
            for half, ref in enumerate(refs):

                def block(i, carry, ref=ref, part=part, half=half):
                    pos = table[span_of(half * ref.shape[0] + i, part)]

                    @pl.when(pos <= limit)
                    def _():
                        key = ref[i, 0]
                        value = ref[i, 1]

                        def head(h, c):
                            at = pl.ds(pl.multiple_of(h * SP, SP), SP)
                            score = lax.dot_general(
                                qs[s, at, :], key, NT, preferred_element_type=jnp.float32
                            )
                            row = lax.broadcasted_iota(jnp.int32, (SP, SP), 0)
                            col = lax.broadcasted_iota(jnp.int32, (SP, SP), 1)
                            keep = (col + pos * SP) <= (row + limit * SP)
                            score = jnp.where(keep, score * SCALE2, -1e30)
                            old = hold[at, :]
                            new = jnp.maximum(old, jnp.max(score, axis=1, keepdims=True))
                            hold[at, :] = new
                            factor = jnp.exp2(old - new)
                            weight = jnp.where(keep, jnp.exp2(score - new), 0.0)
                            acc[s, at, :DH] = acc[s, at, :DH] * factor + jnp.dot(
                                weight.astype(jnp.bfloat16),
                                value,
                                preferred_element_type=jnp.float32,
                            )
                            acc[s, at, DH:] = acc[s, at, DH:] * factor + jnp.sum(
                                weight, axis=1, keepdims=True
                            )
                            return c

                        lax.fori_loop(0, HEADS, head, 0)

                    return carry

                lax.fori_loop(0, ref.shape[0], block, 0)
        for h in range(HEADS):
            at = slice(h * SP, (h + 1) * SP)
            out[s * SP : (s + 1) * SP, h * DH : (h + 1) * DH] = (
                acc[s, at, :DH] / acc[s, at, DH:]
            ).astype(jnp.bfloat16)


def pick_kernel(slots, sa, sb, a_ref, b_ref, pages, sems):
    for part, refs in ((0, (sa, a_ref)), (1, (sb, b_ref))):
        for half, ref in enumerate(refs):

            def block(i, carry, ref=ref, part=part, half=half):
                slot = slots[span_of(half * ref.shape[0] + i, part)]

                @pl.when(slot // 2 == own_ctx())
                def _():
                    j = slot % 2
                    pltpu.make_async_copy(ref.at[i], pages.at[j], sems.at[j]).start()

                return carry

            lax.fori_loop(0, ref.shape[0], block, 0)
    for j in range(2):
        pltpu.make_async_copy(sa.at[0], pages.at[j], sems.at[j]).wait()


def place_kernel(mine, core, zh, other, pages, scales):
    me = lax.axis_index("zh") * 2 + lax.axis_index("core")
    for away, ref in enumerate((mine, core, zh, other)):
        head = me ^ away
        for j in range(2):
            for kind in range(2):
                raw = ref[j, kind].astype(jnp.float32)
                scale = jnp.max(jnp.abs(raw)) + 1e-06
                scales[j, head, kind] = scale
                pages[j, head, kind] = (raw / scale).astype(jnp.bfloat16)


def params():
    return pltpu.CompilerParams(vmem_limit_bytes=56 * 2**20)


def f32(*shape):
    return jax.ShapeDtypeStruct(shape, jnp.float32)


def bf16(*shape):
    return jax.ShapeDtypeStruct(shape, jnp.bfloat16)


def cost(spans):
    return pl.CostEstimate(
        flops=4 * 2 * ROWS * spans * SP * DH * 2,
        transcendentals=2 * ROWS * spans * SP,
        bytes_accessed=8 * 2**20,
    )


def buffers(blocks):
    return [
        pltpu.VMEM((2, ROWS, DH), jnp.bfloat16),
        pltpu.VMEM((2, ROWS, DH), jnp.float32),
        pltpu.VMEM((2, ROWS, 2 * DH), jnp.float32),
        pltpu.VMEM(((blocks + 1) * SP, DH), jnp.bfloat16),
        pltpu.VMEM(((blocks + 1) * SP, 2 * DH), jnp.bfloat16),
        pltpu.SMEM((blocks + 2 * GROUP,), jnp.int32),
        pltpu.SemaphoreType.DMA((3, 2)),
    ]


def swap(x, along_first, mask):
    pairs = []
    for y in range(4):
        for xx in range(4):
            for core in range(2):
                on_x = (core == 0) == along_first
                there = (y, xx ^ mask) if on_x else (y ^ mask, xx)
                pairs.append(((y * 4 + xx) * 2 + core, (there[0] * 4 + there[1]) * 2 + core))
    return lax.ppermute(x, ("y", "x", "core"), pairs)


def on_device(queries, keys, values, span_table, page_slots):
    own = jnp.stack([keys.reshape(2, SP, DH), values.reshape(2, SP, DH)], axis=1)[:, None]
    both = jnp.concatenate([own, lax.ppermute(own, "zl", [(0, 1), (1, 0)])], axis=1)
    held = [both[0], both[1]]
    for stage in range(2):
        come = [swap(held[p], True, MASKS[p][stage]) for p in range(2)]
        held = [jnp.concatenate([held[p], come[p]], axis=0) for p in range(2)]
    come = [swap(held[p], False, MASKS[p][0]) for p in range(2)]
    state = f32(2, ROWS, 2 * DH)
    top, acc1 = pl.pallas_call(
        first_kernel,
        out_shape=(f32(2, ROWS, DH), state),
        in_specs=[SM] + [VM] * 3,
        out_specs=(ANY, ANY),
        scratch_shapes=buffers(16),
        compiler_params=params(),
        cost_estimate=cost(16),
        name="attend_first",
    )(span_table, queries, held[0], held[1])
    more = come
    held = [jnp.concatenate([held[p], come[p]], axis=0) for p in range(2)]
    held[0], held[1], acc1 = lax.optimization_barrier((held[0], held[1], acc1))
    come = [swap(held[p], False, MASKS[p][1]) for p in range(2)]
    acc2 = pl.pallas_call(
        next_kernel,
        out_shape=state,
        in_specs=[SM, VM, ANY, VM, VM],
        out_specs=ANY,
        scratch_shapes=buffers(16),
        compiler_params=params(),
        cost_estimate=cost(16),
        name="attend_next",
    )(span_table, queries, top, more[0], more[1])
    mine = pl.pallas_call(
        pick_kernel,
        out_shape=bf16(2, 2, SP, DH),
        in_specs=[SM] + [ANY] * 4,
        out_specs=ANY,
        scratch_shapes=[pltpu.SemaphoreType.DMA((2,))],
        name="pick_pages",
    )(page_slots, held[0], held[1], come[0], come[1])
    others = [
        lax.ppermute(mine, ("zh", "core"), [(i, i ^ away) for i in range(4)]) for away in (1, 2, 3)
    ]
    attended = pl.pallas_call(
        last_kernel,
        out_shape=bf16(2 * SP, HEADS * DH),
        in_specs=[SM, VM] + [ANY] * 3 + [VM] * 2 + [ANY] * 2,
        out_specs=VM,
        scratch_shapes=buffers(32)
        + [
            pltpu.VMEM((2, ROWS, 2 * DH), jnp.float32),
            pltpu.VMEM((2, ROWS, 2 * DH), jnp.float32),
            pltpu.VMEM((SP, DH), jnp.float32),
            pltpu.VMEM((ROWS, DH), jnp.float32),
            pltpu.VMEM((16, 2, SP, DH), jnp.bfloat16),
            pltpu.VMEM((16, 2, SP, DH), jnp.bfloat16),
            pltpu.SemaphoreType.DMA((2,)),
        ],
        compiler_params=params(),
        cost_estimate=cost(32),
        name="attend_last",
    )(span_table, queries, top, acc1, acc2, come[0], come[1], held[0], held[1])
    pages, scales = pl.pallas_call(
        place_kernel,
        out_shape=(bf16(2, 4, 2, SP, DH), f32(2, 4, 2)),
        in_specs=[VM] * 4,
        out_specs=(VM, SM),
        name="place_pages",
    )(mine, *others)
    return attended, pages, scales


def solution(mesh):
    fine = Mesh(mesh.devices.reshape(4, 2, 4, 2, 2), ("y", "zl", "x", "zh", "core"))
    ctx, page = ("y", "zl", "x"), ("zh", "core")
    return jax.shard_map(
        on_device,
        mesh=fine,
        in_specs=(P(ctx, page), P(ctx, page), P(ctx, page), P(), P()),
        out_specs=(P(ctx, page), P(ctx, None, None, None, None), P(ctx, None, None)),
        check_vma=False,
    )
```

```python
import jax
import jax.numpy as jnp
from jax import lax
from jax.experimental import pallas as pl
from jax.experimental.pallas import tpu as pltpu
from jax.sharding import Mesh, PartitionSpec as P

DH = 128
SP = 128
HEADS = 16
ROWS = HEADS * SP
SCALE2 = DH ** (-0.5) * 1.4426950408889634
TILE = 4
LIMIT = 2.0**100
NT = (((1,), (1,)), ((), ()))
MASKS = ((1, 3), (3, 1))
PIECES = 32
ANY = pl.BlockSpec(memory_space=pl.ANY)
VM = pl.BlockSpec(memory_space=pltpu.VMEM)
SM = pl.BlockSpec(memory_space=pltpu.SMEM)


def tables(span_table, page_slots):
    y, zl, x, core = (lax.axis_index(a) for a in ("y", "zl", "x", "core"))
    index = jnp.arange(2 * PIECES, dtype=jnp.int32)
    part, piece = index // PIECES, index % PIECES
    bit = lambda i: (piece >> i) & 1
    low, high = 1 + 2 * part, 3 - 2 * part
    first = (bit(1) * low) ^ (bit(2) * high)
    second = (bit(3) * low) ^ (bit(4) * high)
    dx = jnp.where(core == 0, first, second)
    dy = jnp.where(core == 0, second, first)
    span = ((y ^ dy) * 8 + (zl ^ bit(0)) * 4 + (x ^ dx)) * 2 + part
    here = span[:, None] == jnp.arange(2 * PIECES, dtype=jnp.int32)[None, :]
    pos = jnp.sum(jnp.where(here, span_table[None, :], 0), axis=1)
    slot = jnp.sum(jnp.where(here, page_slots[None, :], 0), axis=1)
    mine = (y * 8 + zl * 4 + x) * 2 + jnp.arange(2, dtype=jnp.int32)
    want = jnp.sum(jnp.where(slot[None, :] == mine[:, None], index[None, :], 0), axis=1)
    return jnp.concatenate([pos, want])


def rows_of(s):
    return slice(s * SP, (s + 1) * SP)


def queries_of(q_ref, s, tile):
    return jnp.concatenate(
        [q_ref[rows_of(s), (tile * TILE + h) * DH : (tile * TILE + h + 1) * DH] for h in range(TILE)], 0
    )


def blocks_of(table, s, parts):
    limit = table[s * PIECES]
    ks, vs = [], []
    for ref, at in parts:
        for i in range(ref.shape[0]):
            keep = (table[at + i] < limit) | (at + i == s * PIECES)
            flag = jnp.full((SP, DH), keep.astype(jnp.float32)).astype(jnp.bfloat16)
            ks.append(ref[i, 0] * flag)
            vs.append(jnp.concatenate([ref[i, 1] * flag, flag], axis=1))
    return jnp.concatenate(ks, 0), jnp.concatenate(vs, 0), len(ks)


def weigh(score, top, count):
    return jnp.exp2(score * SCALE2 - jnp.concatenate([top] * count, axis=1)).astype(jnp.bfloat16)


def tile_rows(tile):
    return slice(tile * TILE * SP, (tile + 1) * TILE * SP)


def first_kernel(table, q_ref, a_ref, b_ref, top_out, acc_out, top_ref, acc, sems):
    copies = []
    for s in range(2):
        own, other = ((a_ref, 0), (b_ref, PIECES))[:: 1 if s == 0 else -1]
        kg, vg, count = blocks_of(table, s, (own, other))
        for tile in range(HEADS // TILE):
            at = tile_rows(tile)
            score = lax.dot_general(
                queries_of(q_ref, s, tile), kg, NT, preferred_element_type=jnp.float32
            )
            row = lax.broadcasted_iota(jnp.int32, (TILE * SP, SP), 0) % SP
            keep = lax.broadcasted_iota(jnp.int32, (TILE * SP, SP), 1) <= row
            diagonal = jnp.where(keep, score[:, :SP] * SCALE2, -1e30)
            top = jnp.broadcast_to(jnp.max(diagonal, axis=1, keepdims=True), (TILE * SP, SP))
            top_ref[s, at, :] = top
            near = jnp.where(keep, jnp.exp2(diagonal - top), 0.0).astype(jnp.bfloat16)
            weight = jnp.concatenate([near, weigh(score[:, SP:], top, count - 1)], axis=1)
            acc[s, at, :] = jnp.dot(weight, vg, preferred_element_type=jnp.float32)
        for k, (ref, out) in enumerate(((top_ref, top_out), (acc, acc_out))):
            copies.append(pltpu.make_async_copy(ref.at[s], out.at[s], sems.at[k, s]))
            copies[-1].start()
    for copy in copies:
        copy.wait()


def span_sums(s, table, q_ref, parts, top_ref, store):
    kg, vg, count = blocks_of(table, s, parts)
    for tile in range(HEADS // TILE):
        score = lax.dot_general(
            queries_of(q_ref, s, tile), kg, NT, preferred_element_type=jnp.float32
        )
        weight = weigh(score, top_ref[s, tile_rows(tile), :], count)
        store(tile, jnp.dot(weight, vg, preferred_element_type=jnp.float32))


def next_kernel(firsts, table, q_ref, top_in, *refs):
    *pieces, acc_out, top_ref, acc, sems = refs
    parts = tuple(zip(pieces, firsts))
    tops = [pltpu.make_async_copy(top_in.at[s], top_ref.at[s], sems.at[0, s]) for s in range(2)]
    for copy in tops:
        copy.start()
    outs = []
    for s in range(2):
        tops[s].wait()

        def store(tile, sums, s=s):
            acc[s, tile_rows(tile), :] = sums

        span_sums(s, table, q_ref, parts, top_ref, store)
        outs.append(pltpu.make_async_copy(acc.at[s], acc_out.at[s], sems.at[1, s]))
        outs[-1].start()
    for copy in outs:
        copy.wait()


def last_kernel(
    table, q_ref, top_in, acc1_in, acc2_in, acc3_in, b_ref, mine, core, zh, other, sa, sb, ra, rb,
    out, pages, scales,
    top_ref, acc, acc1, acc2, acc3, sems, worst, hold, far_v, far,
):
    ins = ((top_in, top_ref), (acc1_in, acc1), (acc2_in, acc2), (acc3_in, acc3))
    copies = [
        [pltpu.make_async_copy(i.at[s], o.at[s], sems.at[k, s]) for k, (i, o) in enumerate(ins)]
        for s in range(2)
    ]
    for s in range(2):
        for copy in copies[s]:
            copy.start()
    place(mine, core, zh, other, pages, scales)
    worst[...] = jnp.zeros_like(worst)
    for s in range(2):
        for copy in copies[s]:
            copy.wait()

        def store(tile, sums, s=s):
            at = tile_rows(tile)
            both = sums + ((acc1[s, at, :] + acc2[s, at, :]) + acc3[s, at, :])
            total = both[:, DH:]
            worst[...] = jnp.where(total < LIMIT, worst[...], 1.0)
            done = (both[:, :DH] / total).astype(jnp.bfloat16)
            for h in range(TILE):
                head = tile * TILE + h
                out[rows_of(s), head * DH : (head + 1) * DH] = done[rows_of(h)]

        span_sums(s, table, q_ref, ((b_ref, PIECES + PIECES // 2),), top_ref, store)

    @pl.when(jnp.max(worst[...]) > 0.0)
    def _():
        half = PIECES // 2
        fetch = [
            pltpu.make_async_copy(ref, far_v.at[pl.ds(k * half, half)], far.at[k])
            for k, ref in enumerate((sa, ra, sb, rb))
        ]
        for copy in fetch:
            copy.start()
        for copy in fetch:
            copy.wait()
        rescaled(table, q_ref, far_v, out, acc, hold)


def rescaled(table, q_ref, held, out, acc, hold):
    for s in range(2):
        limit = table[s * PIECES]
        hold[...] = jnp.full_like(hold, -1e30)
        acc[...] = jnp.zeros_like(acc)

        def block(i, carry, s=s, limit=limit):
            pos = table[i]

            @pl.when(pos <= limit)
            def _():
                key = held[i, 0]
                value = held[i, 1]

                def head(h, c):
                    at = pl.ds(pl.multiple_of(h * SP, SP), SP)
                    q = q_ref[rows_of(s), pl.ds(pl.multiple_of(h * DH, DH), DH)]
                    score = lax.dot_general(q, key, NT, preferred_element_type=jnp.float32)
                    row = lax.broadcasted_iota(jnp.int32, (SP, SP), 0)
                    col = lax.broadcasted_iota(jnp.int32, (SP, SP), 1)
                    keep = (col + pos * SP) <= (row + limit * SP)
                    score = jnp.where(keep, score * SCALE2, -1e30)
                    old = hold[at, :]
                    new = jnp.maximum(old, jnp.max(score, axis=1, keepdims=True))
                    hold[at, :] = new
                    factor = jnp.exp2(old - new)
                    weight = jnp.where(keep, jnp.exp2(score - new), 0.0)
                    acc[at, :DH] = acc[at, :DH] * factor + jnp.dot(
                        weight.astype(jnp.bfloat16), value, preferred_element_type=jnp.float32
                    )
                    acc[at, DH:] = acc[at, DH:] * factor + jnp.sum(weight, axis=1, keepdims=True)
                    return c

                lax.fori_loop(0, HEADS, head, 0)

            return carry

        lax.fori_loop(0, 2 * PIECES, block, 0)
        for h in range(HEADS):
            out[rows_of(s), h * DH : (h + 1) * DH] = (
                acc[rows_of(h), :DH] / acc[rows_of(h), DH:]
            ).astype(jnp.bfloat16)


def pick_kernel(table, sa, ra, sb, rb, pages, sems):
    half = PIECES // 2
    for j in range(2):
        want = table[2 * PIECES + j]
        for k, ref in enumerate((sa, ra, sb, rb)):

            @pl.when((want >= k * half) & (want < (k + 1) * half))
            def _():
                at = jnp.clip(want - k * half, 0, half - 1)
                pltpu.make_async_copy(ref.at[at], pages.at[j], sems.at[j]).start()

    for j in range(2):
        pltpu.make_async_copy(sa.at[0], pages.at[j], sems.at[j]).wait()


def place(mine, core, zh, other, pages, scales):
    me = lax.axis_index("zh") * 2 + lax.axis_index("core")
    for away, ref in enumerate((mine, core, zh, other)):
        head = me ^ away
        for j in range(2):
            for kind in range(2):
                raw = ref[j, kind].astype(jnp.float32)
                scale = jnp.max(jnp.abs(raw)) + 1e-06
                scales[j, kind, head] = scale
                pages[j, head, kind] = (raw / scale).astype(jnp.bfloat16)


def f32(*shape):
    return jax.ShapeDtypeStruct(shape, jnp.float32)


def bf16(*shape):
    return jax.ShapeDtypeStruct(shape, jnp.bfloat16)


def options():
    return {
        "compiler_params": pltpu.CompilerParams(vmem_limit_bytes=56 * 2**20),
        "cost_estimate": pl.CostEstimate(
            flops=4 * 2 * ROWS * 16 * SP * DH * 2,
            transcendentals=2 * ROWS * 16 * SP,
            bytes_accessed=8 * 2**20,
        ),
    }


TOPS = (2, ROWS, DH)
SUMS = (2, ROWS, 2 * DH)


def sums_of(firsts, name, table, queries, top, *pieces):
    return pl.pallas_call(
        lambda *refs: next_kernel(firsts, *refs),
        out_shape=f32(*SUMS),
        in_specs=[SM, VM, ANY] + [VM] * len(pieces),
        out_specs=ANY,
        scratch_shapes=[
            pltpu.VMEM(TOPS, jnp.float32),
            pltpu.VMEM(SUMS, jnp.float32),
            pltpu.SemaphoreType.DMA((2, 2)),
        ],
        name=name,
        **options(),
    )(table, queries, top, *pieces)


def swap(x, along_first, mask):
    pairs = []
    for y in range(4):
        for xx in range(4):
            for core in range(2):
                on_x = (core == 0) == along_first
                there = (y, xx ^ mask) if on_x else (y ^ mask, xx)
                pairs.append(((y * 4 + xx) * 2 + core, (there[0] * 4 + there[1]) * 2 + core))
    return lax.ppermute(x, ("y", "x", "core"), pairs)


def on_device(queries, keys, values, span_table, page_slots):
    own = jnp.stack([keys.reshape(2, SP, DH), values.reshape(2, SP, DH)], axis=1)[:, None]
    both = jnp.concatenate([own, lax.ppermute(own, "zl", [(0, 1), (1, 0)])], axis=1)
    table = tables(span_table, page_slots)
    held = [both[0], both[1]]
    for stage in range(2):
        come = [swap(held[p], True, MASKS[p][stage]) for p in range(2)]
        held = [jnp.concatenate([held[p], come[p]], axis=0) for p in range(2)]
    come = [swap(held[p], False, MASKS[p][0]) for p in range(2)]
    top, acc1 = pl.pallas_call(
        first_kernel,
        out_shape=(f32(*TOPS), f32(*SUMS)),
        in_specs=[SM] + [VM] * 3,
        out_specs=(ANY, ANY),
        scratch_shapes=[
            pltpu.VMEM(TOPS, jnp.float32),
            pltpu.VMEM(SUMS, jnp.float32),
            pltpu.SemaphoreType.DMA((2, 2)),
        ],
        name="attend_first",
        **options(),
    )(table, queries, held[0], held[1])
    more = come
    held = [jnp.concatenate([held[p], come[p]], axis=0) for p in range(2)]
    held[0], held[1], acc1 = lax.optimization_barrier((held[0], held[1], acc1))
    come = [swap(held[p], False, MASKS[p][1]) for p in range(2)]
    acc2 = sums_of((8, 40), "attend_second", table, queries, top, more[0], more[1])
    mine = pl.pallas_call(
        pick_kernel,
        out_shape=bf16(2, 2, SP, DH),
        in_specs=[SM] + [ANY] * 4,
        out_specs=ANY,
        scratch_shapes=[pltpu.SemaphoreType.DMA((2,))],
        name="pick_pages",
    )(table, held[0], come[0], held[1], come[1])
    others = [
        lax.ppermute(mine, ("zh", "core"), [(i, i ^ away) for i in range(4)]) for away in (1, 2, 3)
    ]
    acc3 = sums_of((16,), "attend_third", table, queries, top, come[0])
    attended, pages, scales = pl.pallas_call(
        last_kernel,
        out_shape=(bf16(2 * SP, HEADS * DH), bf16(2, 4, 2, SP, DH), f32(2, 2, 4)),
        in_specs=[SM, VM] + [ANY] * 4 + [VM] * 5 + [ANY] * 4,
        out_specs=(VM, VM, SM),
        scratch_shapes=[
            pltpu.VMEM(TOPS, jnp.float32),
            pltpu.VMEM((ROWS, 2 * DH), jnp.float32),
            pltpu.VMEM(SUMS, jnp.float32),
            pltpu.VMEM(SUMS, jnp.float32),
            pltpu.VMEM(SUMS, jnp.float32),
            pltpu.SemaphoreType.DMA((4, 2)),
            pltpu.VMEM((TILE * SP, DH), jnp.float32),
            pltpu.VMEM((ROWS, DH), jnp.float32),
            pltpu.VMEM((2 * PIECES, 2, SP, DH), jnp.bfloat16),
            pltpu.SemaphoreType.DMA((4,)),
        ],
        name="attend_last",
        **options(),
    )(
        table, queries, top, acc1, acc2, acc3, come[1], mine, *others,
        held[0], held[1], come[0], come[1],
    )
    return attended, pages, scales.transpose(0, 2, 1)


def solution(mesh):
    fine = Mesh(mesh.devices.reshape(4, 2, 4, 2, 2), ("y", "zl", "x", "zh", "core"))
    ctx, page = ("y", "zl", "x"), ("zh", "core")
    return jax.shard_map(
        on_device,
        mesh=fine,
        in_specs=(P(ctx, page), P(ctx, page), P(ctx, page), P(), P()),
        out_specs=(P(ctx, page), P(ctx, None, None, None, None), P(ctx, None, None)),
        check_vma=False,
    )
```

```python
import jax
import jax.numpy as jnp
from jax import lax
from jax.experimental import pallas as pl
from jax.experimental.pallas import tpu as pltpu
from jax.sharding import Mesh, PartitionSpec as P

DH = 128
SP = 128
HEADS = 16
ROWS = HEADS * SP
SCALE2 = DH ** (-0.5) * 1.4426950408889634
TILE = 4
LIMIT = 2.0**100
NT = (((1,), (1,)), ((), ()))
MASKS = ((1, 3), (3, 1))
PIECES = 32
ANY = pl.BlockSpec(memory_space=pl.ANY)
VM = pl.BlockSpec(memory_space=pltpu.VMEM)
SM = pl.BlockSpec(memory_space=pltpu.SMEM)


def tables(span_table, page_slots):
    y, zl, x, core = (lax.axis_index(a) for a in ("y", "zl", "x", "core"))
    index = jnp.arange(2 * PIECES, dtype=jnp.int32)
    part, piece = index // PIECES, index % PIECES
    bit = lambda i: (piece >> i) & 1
    low, high = 1 + 2 * part, 3 - 2 * part
    first = (bit(1) * low) ^ (bit(2) * high)
    second = (bit(3) * low) ^ (bit(4) * high)
    dx = jnp.where(core == 0, first, second)
    dy = jnp.where(core == 0, second, first)
    span = ((y ^ dy) * 8 + (zl ^ bit(0)) * 4 + (x ^ dx)) * 2 + part
    here = span[:, None] == jnp.arange(2 * PIECES, dtype=jnp.int32)[None, :]
    pos = jnp.sum(jnp.where(here, span_table[None, :], 0), axis=1)
    slot = jnp.sum(jnp.where(here, page_slots[None, :], 0), axis=1)
    mine = (y * 8 + zl * 4 + x) * 2 + jnp.arange(2, dtype=jnp.int32)
    want = jnp.sum(jnp.where(slot[None, :] == mine[:, None], index[None, :], 0), axis=1)
    return jnp.concatenate([pos, want])


def rows_of(s):
    return pl.ds(s * SP, SP)


def queries_of(q_ref, s, tile):
    rows = pl.ds(pl.multiple_of(s * SP, SP), SP)
    return jnp.concatenate(
        [q_ref[rows, (tile * TILE + h) * DH : (tile * TILE + h + 1) * DH] for h in range(TILE)], 0
    )


def kept(key, value, keep):
    flag = jnp.full((SP, DH), keep.astype(jnp.float32)).astype(jnp.bfloat16)
    return key * flag, jnp.concatenate([value * flag, flag], axis=1)


def blocks_of(table, s, parts, skip=0):
    limit = table[s * PIECES]
    ks, vs = [], []
    for ref, at in parts:
        for i in range(skip, ref.shape[0]):
            key, value = kept(ref[i, 0], ref[i, 1], table[at + i] < limit)
            ks.append(key)
            vs.append(value)
    return ks, vs


def weigh(score, top, count):
    return jnp.exp2(score * SCALE2 - jnp.concatenate([top] * count, axis=1)).astype(jnp.bfloat16)


def tile_rows(tile):
    return slice(tile * TILE * SP, (tile + 1) * TILE * SP)


def first_kernel(table, q_ref, a_ref, b_ref, top_out, acc_out, top_ref, acc, sems):
    def span(s, carry):
        swapped = jnp.full((2, SP, DH), s) > 0
        own = jnp.where(swapped, b_ref[0], a_ref[0])
        other = jnp.where(swapped, a_ref[0], b_ref[0])
        near_first = table[(1 - s) * PIECES] < table[s * PIECES]
        ks, vs = blocks_of(table, s, ((a_ref, 0), (b_ref, PIECES)), 1)
        key, value = kept(other[0], other[1], near_first)
        ones = jnp.ones((SP, DH), jnp.bfloat16)
        kg = jnp.concatenate([own[0], key] + ks, 0)
        vg = jnp.concatenate([jnp.concatenate([own[1], ones], axis=1), value] + vs, 0)
        for tile in range(HEADS // TILE):
            at = tile_rows(tile)
            score = lax.dot_general(
                queries_of(q_ref, s, tile), kg, NT, preferred_element_type=jnp.float32
            )
            row = lax.broadcasted_iota(jnp.int32, (TILE * SP, SP), 0) % SP
            keep = lax.broadcasted_iota(jnp.int32, (TILE * SP, SP), 1) <= row
            diagonal = jnp.where(keep, score[:, :SP] * SCALE2, -1e30)
            top = jnp.broadcast_to(jnp.max(diagonal, axis=1, keepdims=True), (TILE * SP, SP))
            top_ref[s, at, :] = top
            near = jnp.where(keep, jnp.exp2(diagonal - top), 0.0).astype(jnp.bfloat16)
            weight = jnp.concatenate([near, weigh(score[:, SP:], top, len(ks) + 1)], axis=1)
            acc[s, at, :] = jnp.dot(weight, vg, preferred_element_type=jnp.float32)
        for k, (ref, out) in enumerate(((top_ref, top_out), (acc, acc_out))):
            pltpu.make_async_copy(ref.at[s], out.at[s], sems.at[k, s]).start()
        return carry

    lax.fori_loop(0, 2, span, 0)
    for s in range(2):
        for k, (ref, out) in enumerate(((top_ref, top_out), (acc, acc_out))):
            pltpu.make_async_copy(ref.at[s], out.at[s], sems.at[k, s]).wait()


def span_sums(s, table, q_ref, parts, top_ref, store):
    ks, vs = blocks_of(table, s, parts)
    kg, vg = jnp.concatenate(ks, 0), jnp.concatenate(vs, 0)
    for tile in range(HEADS // TILE):
        score = lax.dot_general(
            queries_of(q_ref, s, tile), kg, NT, preferred_element_type=jnp.float32
        )
        weight = weigh(score, top_ref[s, tile_rows(tile), :], len(ks))
        store(tile, jnp.dot(weight, vg, preferred_element_type=jnp.float32))


def next_kernel(firsts, table, q_ref, top_in, *refs):
    *pieces, acc_out, top_ref, acc, sems = refs
    parts = tuple(zip(pieces, firsts))
    for s in range(2):
        pltpu.make_async_copy(top_in.at[s], top_ref.at[s], sems.at[0, s]).start()

    def span(s, carry):
        pltpu.make_async_copy(top_in.at[s], top_ref.at[s], sems.at[0, s]).wait()

        def store(tile, sums):
            acc[s, tile_rows(tile), :] = sums

        span_sums(s, table, q_ref, parts, top_ref, store)
        pltpu.make_async_copy(acc.at[s], acc_out.at[s], sems.at[1, s]).start()
        return carry

    lax.fori_loop(0, 2, span, 0)
    for s in range(2):
        pltpu.make_async_copy(acc.at[s], acc_out.at[s], sems.at[1, s]).wait()


def last_kernel(
    table, q_ref, top_in, acc1_in, acc2_in, acc3_in, b_ref, mine, core, zh, other, sa, sb, ra, rb,
    out, pages, scales,
    top_ref, acc, acc1, acc2, acc3, sems, worst, hold, far_v, far,
):
    ins = ((top_in, top_ref), (acc1_in, acc1), (acc2_in, acc2), (acc3_in, acc3))
    for s in range(2):
        for k, (i, o) in enumerate(ins):
            pltpu.make_async_copy(i.at[s], o.at[s], sems.at[k, s]).start()
    place(mine, core, zh, other, pages, scales)
    worst[...] = jnp.zeros_like(worst)

    def span(s, carry):
        for k, (i, o) in enumerate(ins):
            pltpu.make_async_copy(i.at[s], o.at[s], sems.at[k, s]).wait()

        def store(tile, sums):
            at = tile_rows(tile)
            both = sums + ((acc1[s, at, :] + acc2[s, at, :]) + acc3[s, at, :])
            total = both[:, DH:]
            worst[...] = jnp.where(total < LIMIT, worst[...], 1.0)
            done = (both[:, :DH] / total).astype(jnp.bfloat16)
            for h in range(TILE):
                head = tile * TILE + h
                rows = pl.ds(pl.multiple_of(s * SP, SP), SP)
                out[rows, head * DH : (head + 1) * DH] = done[h * SP : (h + 1) * SP]

        span_sums(s, table, q_ref, ((b_ref, PIECES + PIECES // 2),), top_ref, store)
        return carry

    lax.fori_loop(0, 2, span, 0)

    @pl.when(jnp.max(worst[...]) > 0.0)
    def _():
        half = PIECES // 2
        fetch = [
            pltpu.make_async_copy(ref, far_v.at[pl.ds(k * half, half)], far.at[k])
            for k, ref in enumerate((sa, ra, sb, rb))
        ]
        for copy in fetch:
            copy.start()
        for copy in fetch:
            copy.wait()
        rescaled(table, q_ref, far_v, out, acc, hold)


def rescaled(table, q_ref, held, out, acc, hold):
    for s in range(2):
        limit = table[s * PIECES]
        hold[...] = jnp.full_like(hold, -1e30)
        acc[...] = jnp.zeros_like(acc)

        def block(i, carry, s=s, limit=limit):
            pos = table[i]

            @pl.when(pos <= limit)
            def _():
                key = held[i, 0]
                value = held[i, 1]

                def head(h, c):
                    at = pl.ds(pl.multiple_of(h * SP, SP), SP)
                    q = q_ref[rows_of(s), pl.ds(pl.multiple_of(h * DH, DH), DH)]
                    score = lax.dot_general(q, key, NT, preferred_element_type=jnp.float32)
                    row = lax.broadcasted_iota(jnp.int32, (SP, SP), 0)
                    col = lax.broadcasted_iota(jnp.int32, (SP, SP), 1)
                    keep = (col + pos * SP) <= (row + limit * SP)
                    score = jnp.where(keep, score * SCALE2, -1e30)
                    old = hold[at, :]
                    new = jnp.maximum(old, jnp.max(score, axis=1, keepdims=True))
                    hold[at, :] = new
                    factor = jnp.exp2(old - new)
                    weight = jnp.where(keep, jnp.exp2(score - new), 0.0)
                    acc[at, :DH] = acc[at, :DH] * factor + jnp.dot(
                        weight.astype(jnp.bfloat16), value, preferred_element_type=jnp.float32
                    )
                    acc[at, DH:] = acc[at, DH:] * factor + jnp.sum(weight, axis=1, keepdims=True)
                    return c

                lax.fori_loop(0, HEADS, head, 0)

            return carry

        lax.fori_loop(0, 2 * PIECES, block, 0)
        for h in range(HEADS):
            out[rows_of(s), h * DH : (h + 1) * DH] = (
                acc[rows_of(h), :DH] / acc[rows_of(h), DH:]
            ).astype(jnp.bfloat16)


def pick_kernel(table, sa, ra, sb, rb, pages, sems):
    half = PIECES // 2
    for j in range(2):
        want = table[2 * PIECES + j]
        for k, ref in enumerate((sa, ra, sb, rb)):

            @pl.when((want >= k * half) & (want < (k + 1) * half))
            def _():
                at = jnp.clip(want - k * half, 0, half - 1)
                pltpu.make_async_copy(ref.at[at], pages.at[j], sems.at[j]).start()

    for j in range(2):
        pltpu.make_async_copy(sa.at[0], pages.at[j], sems.at[j]).wait()


def place(mine, core, zh, other, pages, scales):
    me = lax.axis_index("zh") * 2 + lax.axis_index("core")
    lane = lax.broadcasted_iota(jnp.int32, (1, 4), 1)
    for j in range(2):
        for kind in range(2):
            row = jnp.zeros((1, 4), jnp.float32)
            for away, ref in enumerate((mine, core, zh, other)):
                head = me ^ away
                raw = ref[j, kind].astype(jnp.float32)
                high = jnp.max(jnp.abs(raw), axis=0, keepdims=True)
                scale = jnp.max(high, axis=1, keepdims=True) + 1e-06
                row = jnp.where(lane == head, scale, row)
                pages[j, head, kind] = (raw / scale).astype(jnp.bfloat16)
            scales[j, kind : kind + 1, :] = row


def f32(*shape):
    return jax.ShapeDtypeStruct(shape, jnp.float32)


def bf16(*shape):
    return jax.ShapeDtypeStruct(shape, jnp.bfloat16)


def options():
    return {
        "compiler_params": pltpu.CompilerParams(vmem_limit_bytes=56 * 2**20),
        "cost_estimate": pl.CostEstimate(
            flops=4 * 2 * ROWS * 16 * SP * DH * 2,
            transcendentals=2 * ROWS * 16 * SP,
            bytes_accessed=8 * 2**20,
        ),
    }


TOPS = (2, ROWS, DH)
SUMS = (2, ROWS, 2 * DH)


def sums_of(firsts, name, table, queries, top, *pieces):
    return pl.pallas_call(
        lambda *refs: next_kernel(firsts, *refs),
        out_shape=f32(*SUMS),
        in_specs=[SM, VM, ANY] + [VM] * len(pieces),
        out_specs=ANY,
        scratch_shapes=[
            pltpu.VMEM(TOPS, jnp.float32),
            pltpu.VMEM(SUMS, jnp.float32),
            pltpu.SemaphoreType.DMA((2, 2)),
        ],
        name=name,
        **options(),
    )(table, queries, top, *pieces)


def swap(x, along_first, mask):
    pairs = []
    for y in range(4):
        for xx in range(4):
            for core in range(2):
                on_x = (core == 0) == along_first
                there = (y, xx ^ mask) if on_x else (y ^ mask, xx)
                pairs.append(((y * 4 + xx) * 2 + core, (there[0] * 4 + there[1]) * 2 + core))
    return lax.ppermute(x, ("y", "x", "core"), pairs)


def on_device(queries, keys, values, span_table, page_slots):
    own = jnp.stack([keys.reshape(2, SP, DH), values.reshape(2, SP, DH)], axis=1)[:, None]
    both = jnp.concatenate([own, lax.ppermute(own, "zl", [(0, 1), (1, 0)])], axis=1)
    table = tables(span_table, page_slots)
    held = [both[0], both[1]]
    for stage in range(2):
        come = [swap(held[p], True, MASKS[p][stage]) for p in range(2)]
        held = [jnp.concatenate([held[p], come[p]], axis=0) for p in range(2)]
    come = [swap(held[p], False, MASKS[p][0]) for p in range(2)]
    top, acc1 = pl.pallas_call(
        first_kernel,
        out_shape=(f32(*TOPS), f32(*SUMS)),
        in_specs=[SM] + [VM] * 3,
        out_specs=(ANY, ANY),
        scratch_shapes=[
            pltpu.VMEM(TOPS, jnp.float32),
            pltpu.VMEM(SUMS, jnp.float32),
            pltpu.SemaphoreType.DMA((2, 2)),
        ],
        name="attend_first",
        **options(),
    )(table, queries, held[0], held[1])
    more = come
    held = [jnp.concatenate([held[p], come[p]], axis=0) for p in range(2)]
    held[0], held[1], acc1 = lax.optimization_barrier((held[0], held[1], acc1))
    come = [swap(held[p], False, MASKS[p][1]) for p in range(2)]
    acc2 = sums_of((8, 40), "attend_second", table, queries, top, more[0], more[1])
    mine = pl.pallas_call(
        pick_kernel,
        out_shape=bf16(2, 2, SP, DH),
        in_specs=[SM] + [ANY] * 4,
        out_specs=VM,
        scratch_shapes=[pltpu.SemaphoreType.DMA((2,))],
        name="pick_pages",
    )(table, held[0], come[0], held[1], come[1])
    others = [
        lax.ppermute(mine, ("zh", "core"), [(i, i ^ away) for i in range(4)]) for away in (1, 2, 3)
    ]
    acc3 = sums_of((16,), "attend_third", table, queries, top, come[0])
    attended, pages, scales = pl.pallas_call(
        last_kernel,
        out_shape=(bf16(2 * SP, HEADS * DH), bf16(2, 4, 2, SP, DH), f32(2, 2, 4)),
        in_specs=[SM, VM] + [ANY] * 4 + [VM] * 5 + [ANY] * 4,
        out_specs=(VM, VM, VM),
        scratch_shapes=[
            pltpu.VMEM(TOPS, jnp.float32),
            pltpu.VMEM((ROWS, 2 * DH), jnp.float32),
            pltpu.VMEM(SUMS, jnp.float32),
            pltpu.VMEM(SUMS, jnp.float32),
            pltpu.VMEM(SUMS, jnp.float32),
            pltpu.SemaphoreType.DMA((4, 2)),
            pltpu.VMEM((TILE * SP, DH), jnp.float32),
            pltpu.VMEM((ROWS, DH), jnp.float32),
            pltpu.VMEM((2 * PIECES, 2, SP, DH), jnp.bfloat16),
            pltpu.SemaphoreType.DMA((4,)),
        ],
        name="attend_last",
        **options(),
    )(
        table, queries, top, acc1, acc2, acc3, come[1], mine, *others,
        held[0], held[1], come[0], come[1],
    )
    return attended, pages, scales.transpose(0, 2, 1)


def solution(mesh):
    fine = Mesh(mesh.devices.reshape(4, 2, 4, 2, 2), ("y", "zl", "x", "zh", "core"))
    ctx, page = ("y", "zl", "x"), ("zh", "core")
    return jax.shard_map(
        on_device,
        mesh=fine,
        in_specs=(P(ctx, page), P(ctx, page), P(ctx, page), P(), P()),
        out_specs=(P(ctx, page), P(ctx, None, None, None, None), P(ctx, None, None)),
        check_vma=False,
    )
```

```python
import jax
import jax.numpy as jnp
from jax import lax
from jax.experimental import pallas as pl
from jax.experimental.pallas import tpu as pltpu
from jax.sharding import Mesh, PartitionSpec as P

DH = 128
SP = 128
HEADS = 16
ROWS = HEADS * SP
SCALE2 = DH ** (-0.5) * 1.4426950408889634
TILE = 4
LIMIT = 2.0**100
NT = (((1,), (1,)), ((), ()))
MASKS = ((1, 3), (3, 1))
PIECES = 32
ANY = pl.BlockSpec(memory_space=pl.ANY)
VM = pl.BlockSpec(memory_space=pltpu.VMEM)
SM = pl.BlockSpec(memory_space=pltpu.SMEM)


def tables(span_table, page_slots):
    y, zl, x, core = (lax.axis_index(a) for a in ("y", "zl", "x", "core"))
    index = jnp.arange(2 * PIECES, dtype=jnp.int32)
    part, piece = index // PIECES, index % PIECES
    bit = lambda i: (piece >> i) & 1
    low, high = 1 + 2 * part, 3 - 2 * part
    first = (bit(1) * low) ^ (bit(2) * high)
    second = (bit(3) * low) ^ (bit(4) * high)
    dx = jnp.where(core == 0, first, second)
    dy = jnp.where(core == 0, second, first)
    span = ((y ^ dy) * 8 + (zl ^ bit(0)) * 4 + (x ^ dx)) * 2 + part
    here = span[:, None] == jnp.arange(2 * PIECES, dtype=jnp.int32)[None, :]
    pos = jnp.sum(jnp.where(here, span_table[None, :], 0), axis=1)
    slot = jnp.sum(jnp.where(here, page_slots[None, :], 0), axis=1)
    mine = (y * 8 + zl * 4 + x) * 2 + jnp.arange(2, dtype=jnp.int32)
    want = jnp.sum(jnp.where(slot[None, :] == mine[:, None], index[None, :], 0), axis=1)
    return jnp.concatenate([pos, want])


def rows_of(s):
    return pl.ds(s * SP, SP)


def queries_of(q_ref, s, tile):
    rows = pl.ds(pl.multiple_of(s * SP, SP), SP)
    return jnp.concatenate(
        [q_ref[rows, (tile * TILE + h) * DH : (tile * TILE + h + 1) * DH] for h in range(TILE)], 0
    )


def kept(key, value, keep):
    flag = jnp.full((SP, DH), keep.astype(jnp.float32)).astype(jnp.bfloat16)
    return key * flag, jnp.concatenate([value * flag, flag], axis=1)


def blocks_of(table, s, parts, skip=0):
    limit = table[s * PIECES]
    ks, vs = [], []
    for ref, at in parts:
        for i in range(skip, ref.shape[0]):
            key, value = kept(ref[i, 0], ref[i, 1], table[at + i] < limit)
            ks.append(key)
            vs.append(value)
    return ks, vs


def weigh(score, top, count):
    return jnp.exp2(score * SCALE2 - jnp.concatenate([top] * count, axis=1)).astype(jnp.bfloat16)


def tile_rows(tile):
    return slice(tile * TILE * SP, (tile + 1) * TILE * SP)


def first_kernel(table, q_ref, a_ref, b_ref, top_out, acc_out, top_ref, acc, sems):
    def span(s, carry):
        swapped = jnp.full((2, SP, DH), s) > 0
        own = jnp.where(swapped, b_ref[0], a_ref[0])
        other = jnp.where(swapped, a_ref[0], b_ref[0])
        near_first = table[(1 - s) * PIECES] < table[s * PIECES]
        ks, vs = blocks_of(table, s, ((a_ref, 0), (b_ref, PIECES)), 1)
        key, value = kept(other[0], other[1], near_first)
        ones = jnp.ones((SP, DH), jnp.bfloat16)
        kg = jnp.concatenate([own[0], key] + ks, 0)
        vg = jnp.concatenate([jnp.concatenate([own[1], ones], axis=1), value] + vs, 0)
        for tile in range(HEADS // TILE):
            at = tile_rows(tile)
            score = lax.dot_general(
                queries_of(q_ref, s, tile), kg, NT, preferred_element_type=jnp.float32
            )
            row = lax.broadcasted_iota(jnp.int32, (TILE * SP, SP), 0) % SP
            keep = lax.broadcasted_iota(jnp.int32, (TILE * SP, SP), 1) <= row
            diagonal = jnp.where(keep, score[:, :SP] * SCALE2, -1e30)
            top = jnp.broadcast_to(jnp.max(diagonal, axis=1, keepdims=True), (TILE * SP, SP))
            top_ref[s, at, :] = top
            near = jnp.where(keep, jnp.exp2(diagonal - top), 0.0).astype(jnp.bfloat16)
            weight = jnp.concatenate([near, weigh(score[:, SP:], top, len(ks) + 1)], axis=1)
            acc[s, at, :] = jnp.dot(weight, vg, preferred_element_type=jnp.float32)
        for k, (ref, out) in enumerate(((top_ref, top_out), (acc, acc_out))):
            pltpu.make_async_copy(ref.at[s], out.at[s], sems.at[k, s]).start()
        return carry

    lax.fori_loop(0, 2, span, 0)
    for s in range(2):
        for k, (ref, out) in enumerate(((top_ref, top_out), (acc, acc_out))):
            pltpu.make_async_copy(ref.at[s], out.at[s], sems.at[k, s]).wait()


def span_sums(s, table, q_ref, parts, top_ref, store):
    ks, vs = blocks_of(table, s, parts)
    kg, vg = jnp.concatenate(ks, 0), jnp.concatenate(vs, 0)
    for tile in range(HEADS // TILE):
        score = lax.dot_general(
            queries_of(q_ref, s, tile), kg, NT, preferred_element_type=jnp.float32
        )
        weight = weigh(score, top_ref[s, tile_rows(tile), :], len(ks))
        store(tile, jnp.dot(weight, vg, preferred_element_type=jnp.float32))


def next_kernel(firsts, table, q_ref, top_in, acc_in, *refs):
    *pieces, acc_out, top_ref, acc, sems = refs
    parts = tuple(zip(pieces, firsts))
    ins = ((top_in, top_ref), (acc_in, acc))
    for s in range(2):
        for k, (i, o) in enumerate(ins):
            pltpu.make_async_copy(i.at[s], o.at[s], sems.at[k, s]).start()

    def span(s, carry):
        for k, (i, o) in enumerate(ins):
            pltpu.make_async_copy(i.at[s], o.at[s], sems.at[k, s]).wait()

        def store(tile, sums):
            at = tile_rows(tile)
            acc[s, at, :] = acc[s, at, :] + sums

        span_sums(s, table, q_ref, parts, top_ref, store)
        pltpu.make_async_copy(acc.at[s], acc_out.at[s], sems.at[2, s]).start()
        return carry

    lax.fori_loop(0, 2, span, 0)
    for s in range(2):
        pltpu.make_async_copy(acc.at[s], acc_out.at[s], sems.at[2, s]).wait()


def last_kernel(
    table, q_ref, top_in, acc_in, b_ref, mine, core, zh, other, sa, sb, ra, rb,
    out, pages, scales,
    top_ref, acc, hold, sems, worst, far_v, far,
):
    ins = ((top_in, top_ref), (acc_in, acc))
    for s in range(2):
        for k, (i, o) in enumerate(ins):
            pltpu.make_async_copy(i.at[s], o.at[s], sems.at[k, s]).start()
    place(mine, core, zh, other, pages, scales)
    worst[...] = jnp.zeros_like(worst)

    def span(s, carry):
        for k, (i, o) in enumerate(ins):
            pltpu.make_async_copy(i.at[s], o.at[s], sems.at[k, s]).wait()

        def store(tile, sums):
            at = tile_rows(tile)
            both = acc[s, at, :] + sums
            total = both[:, DH:]
            worst[...] = jnp.where(total < LIMIT, worst[...], 1.0)
            done = (both[:, :DH] / total).astype(jnp.bfloat16)
            for h in range(TILE):
                head = tile * TILE + h
                rows = pl.ds(pl.multiple_of(s * SP, SP), SP)
                out[rows, head * DH : (head + 1) * DH] = done[h * SP : (h + 1) * SP]

        span_sums(s, table, q_ref, ((b_ref, PIECES + PIECES // 2),), top_ref, store)
        return carry

    lax.fori_loop(0, 2, span, 0)

    @pl.when(jnp.max(worst[...]) > 0.0)
    def _():
        half = PIECES // 2
        fetch = [
            pltpu.make_async_copy(ref, far_v.at[pl.ds(k * half, half)], far.at[k])
            for k, ref in enumerate((sa, ra, sb, rb))
        ]
        for copy in fetch:
            copy.start()
        for copy in fetch:
            copy.wait()
        rescaled(table, q_ref, far_v, out, acc.at[0], hold)


def rescaled(table, q_ref, held, out, acc, hold):
    for s in range(2):
        limit = table[s * PIECES]
        hold[...] = jnp.full_like(hold, -1e30)
        acc[...] = jnp.zeros_like(acc)

        def block(i, carry, s=s, limit=limit):
            pos = table[i]

            @pl.when(pos <= limit)
            def _():
                key = held[i, 0]
                value = held[i, 1]

                def head(h, c):
                    at = pl.ds(pl.multiple_of(h * SP, SP), SP)
                    q = q_ref[rows_of(s), pl.ds(pl.multiple_of(h * DH, DH), DH)]
                    score = lax.dot_general(q, key, NT, preferred_element_type=jnp.float32)
                    row = lax.broadcasted_iota(jnp.int32, (SP, SP), 0)
                    col = lax.broadcasted_iota(jnp.int32, (SP, SP), 1)
                    keep = (col + pos * SP) <= (row + limit * SP)
                    score = jnp.where(keep, score * SCALE2, -1e30)
                    old = hold[at, :]
                    new = jnp.maximum(old, jnp.max(score, axis=1, keepdims=True))
                    hold[at, :] = new
                    factor = jnp.exp2(old - new)
                    weight = jnp.where(keep, jnp.exp2(score - new), 0.0)
                    acc[at, :DH] = acc[at, :DH] * factor + jnp.dot(
                        weight.astype(jnp.bfloat16), value, preferred_element_type=jnp.float32
                    )
                    acc[at, DH:] = acc[at, DH:] * factor + jnp.sum(weight, axis=1, keepdims=True)
                    return c

                lax.fori_loop(0, HEADS, head, 0)

            return carry

        lax.fori_loop(0, 2 * PIECES, block, 0)
        for h in range(HEADS):
            out[rows_of(s), h * DH : (h + 1) * DH] = (
                acc[rows_of(h), :DH] / acc[rows_of(h), DH:]
            ).astype(jnp.bfloat16)


def pick_kernel(table, sa, ra, sb, rb, pages, sems):
    half = PIECES // 2
    for j in range(2):
        want = table[2 * PIECES + j]
        for k, ref in enumerate((sa, ra, sb, rb)):

            @pl.when((want >= k * half) & (want < (k + 1) * half))
            def _():
                at = jnp.clip(want - k * half, 0, half - 1)
                pltpu.make_async_copy(ref.at[at], pages.at[j], sems.at[j]).start()

    for j in range(2):
        pltpu.make_async_copy(sa.at[0], pages.at[j], sems.at[j]).wait()


def place(mine, core, zh, other, pages, scales):
    me = lax.axis_index("zh") * 2 + lax.axis_index("core")
    lane = lax.broadcasted_iota(jnp.int32, (1, 4), 1)
    for j in range(2):
        for kind in range(2):
            row = jnp.zeros((1, 4), jnp.float32)
            for away, ref in enumerate((mine, core, zh, other)):
                head = me ^ away
                raw = ref[j, kind].astype(jnp.float32)
                high = jnp.max(jnp.abs(raw), axis=0, keepdims=True)
                scale = jnp.max(high, axis=1, keepdims=True) + 1e-06
                row = jnp.where(lane == head, scale, row)
                pages[j, head, kind] = (raw / scale).astype(jnp.bfloat16)
            scales[j, kind : kind + 1, :] = row


def f32(*shape):
    return jax.ShapeDtypeStruct(shape, jnp.float32)


def bf16(*shape):
    return jax.ShapeDtypeStruct(shape, jnp.bfloat16)


def options(spans):
    return {
        "compiler_params": pltpu.CompilerParams(vmem_limit_bytes=56 * 2**20),
        "cost_estimate": pl.CostEstimate(
            flops=4 * 2 * ROWS * spans * SP * DH * 2,
            transcendentals=2 * ROWS * spans * SP,
            bytes_accessed=8 * 2**20,
        ),
    }


TOPS = (2, ROWS, DH)
SUMS = (2, ROWS, 2 * DH)


def state():
    return [
        pltpu.VMEM(TOPS, jnp.float32),
        pltpu.VMEM(SUMS, jnp.float32),
        pltpu.SemaphoreType.DMA((3, 2)),
    ]


def sums_of(firsts, name, table, queries, top, acc, *pieces):
    return pl.pallas_call(
        lambda *refs: next_kernel(firsts, *refs),
        out_shape=f32(*SUMS),
        in_specs=[SM, VM, ANY, ANY] + [VM] * len(pieces),
        out_specs=ANY,
        scratch_shapes=state(),
        name=name,
        **options(sum(p.shape[0] for p in pieces)),
    )(table, queries, top, acc, *pieces)


def swap(x, along_first, mask):
    pairs = []
    for y in range(4):
        for xx in range(4):
            for core in range(2):
                on_x = (core == 0) == along_first
                there = (y, xx ^ mask) if on_x else (y ^ mask, xx)
                pairs.append(((y * 4 + xx) * 2 + core, (there[0] * 4 + there[1]) * 2 + core))
    return lax.ppermute(x, ("y", "x", "core"), pairs)


def on_device(queries, keys, values, span_table, page_slots):
    own = jnp.stack([keys.reshape(2, SP, DH), values.reshape(2, SP, DH)], axis=1)[:, None]
    both = jnp.concatenate([own, lax.ppermute(own, "zl", [(0, 1), (1, 0)])], axis=1)
    table = tables(span_table, page_slots)
    held = [both[0], both[1]]

    def exchange(held, along_first, stage):
        return [swap(held[p], along_first, MASKS[p][stage]) for p in range(2)]

    def grown(held, come):
        return [jnp.concatenate([held[p], come[p]], axis=0) for p in range(2)]

    held = grown(held, exchange(held, True, 0))
    come = exchange(held, True, 1)
    top, acc = pl.pallas_call(
        first_kernel,
        out_shape=(f32(*TOPS), f32(*SUMS)),
        in_specs=[SM] + [VM] * 3,
        out_specs=(ANY, ANY),
        scratch_shapes=state(),
        name="attend_first",
        **options(8),
    )(table, queries, held[0], held[1])
    for stage in range(2):
        more = come
        held = grown(held, come)
        held[0], held[1], acc = lax.optimization_barrier((held[0], held[1], acc))
        come = exchange(held, False, stage)
        at = 4 << stage
        acc = sums_of(
            (at, PIECES + at), ("attend_second", "attend_third")[stage], table, queries, top, acc, *more
        )
    mine = pl.pallas_call(
        pick_kernel,
        out_shape=bf16(2, 2, SP, DH),
        in_specs=[SM] + [ANY] * 4,
        out_specs=VM,
        scratch_shapes=[pltpu.SemaphoreType.DMA((2,))],
        name="pick_pages",
    )(table, held[0], come[0], held[1], come[1])
    others = [
        lax.ppermute(mine, ("zh", "core"), [(i, i ^ away) for i in range(4)]) for away in (1, 2, 3)
    ]
    acc = sums_of((16,), "attend_fourth", table, queries, top, acc, come[0])
    attended, pages, scales = pl.pallas_call(
        last_kernel,
        out_shape=(bf16(2 * SP, HEADS * DH), bf16(2, 4, 2, SP, DH), f32(2, 2, 4)),
        in_specs=[SM, VM] + [ANY] * 2 + [VM] * 5 + [ANY] * 4,
        out_specs=(VM, VM, VM),
        scratch_shapes=[
            pltpu.VMEM(TOPS, jnp.float32),
            pltpu.VMEM(SUMS, jnp.float32),
            pltpu.VMEM((ROWS, DH), jnp.float32),
            pltpu.SemaphoreType.DMA((2, 2)),
            pltpu.VMEM((TILE * SP, DH), jnp.float32),
            pltpu.VMEM((2 * PIECES, 2, SP, DH), jnp.bfloat16),
            pltpu.SemaphoreType.DMA((4,)),
        ],
        name="attend_last",
        **options(16),
    )(
        table, queries, top, acc, come[1], mine, *others,
        held[0], held[1], come[0], come[1],
    )
    return attended, pages, scales.transpose(0, 2, 1)


def solution(mesh):
    fine = Mesh(mesh.devices.reshape(4, 2, 4, 2, 2), ("y", "zl", "x", "zh", "core"))
    ctx, page = ("y", "zl", "x"), ("zh", "core")
    return jax.shard_map(
        on_device,
        mesh=fine,
        in_specs=(P(ctx, page), P(ctx, page), P(ctx, page), P(), P()),
        out_specs=(P(ctx, page), P(ctx, None, None, None, None), P(ctx, None, None)),
        check_vma=False,
    )
```

```python
import jax
import jax.numpy as jnp
from jax import lax
from jax.experimental import pallas as pl
from jax.experimental.pallas import tpu as pltpu
from jax.sharding import Mesh, PartitionSpec as P

DH = 128
SP = 128
HEADS = 16
ROWS = HEADS * SP
SCALE2 = DH ** (-0.5) * 1.4426950408889634
TILE = 4
LIMIT = 2.0**100
FRONT = pl.ds(0, ROWS - TILE * SP)
BACK = pl.ds(ROWS - TILE * SP, TILE * SP)
NT = (((1,), (1,)), ((), ()))
MASKS = ((1, 3), (3, 1))
PIECES = 32
ANY = pl.BlockSpec(memory_space=pl.ANY)
VM = pl.BlockSpec(memory_space=pltpu.VMEM)
SM = pl.BlockSpec(memory_space=pltpu.SMEM)


def tables(span_table, page_slots):
    y, zl, x, core = (lax.axis_index(a) for a in ("y", "zl", "x", "core"))
    index = jnp.arange(2 * PIECES, dtype=jnp.int32)
    part, piece = index // PIECES, index % PIECES
    bit = lambda i: (piece >> i) & 1
    low, high = 1 + 2 * part, 3 - 2 * part
    first = (bit(1) * low) ^ (bit(2) * high)
    second = (bit(3) * low) ^ (bit(4) * high)
    dx = jnp.where(core == 0, first, second)
    dy = jnp.where(core == 0, second, first)
    span = ((y ^ dy) * 8 + (zl ^ bit(0)) * 4 + (x ^ dx)) * 2 + part
    here = span[:, None] == jnp.arange(2 * PIECES, dtype=jnp.int32)[None, :]
    pos = jnp.sum(jnp.where(here, span_table[None, :], 0), axis=1)
    slot = jnp.sum(jnp.where(here, page_slots[None, :], 0), axis=1)
    mine = (y * 8 + zl * 4 + x) * 2 + jnp.arange(2, dtype=jnp.int32)
    want = jnp.sum(jnp.where(slot[None, :] == mine[:, None], index[None, :], 0), axis=1)
    return jnp.concatenate([pos, want])


def rows_of(s):
    return pl.ds(s * SP, SP)


def queries_of(q_ref, s, tile):
    rows = pl.ds(pl.multiple_of(s * SP, SP), SP)
    return jnp.concatenate(
        [q_ref[rows, (tile * TILE + h) * DH : (tile * TILE + h + 1) * DH] for h in range(TILE)], 0
    )


def kept(key, value, keep):
    flag = jnp.full((SP, DH), keep.astype(jnp.float32)).astype(jnp.bfloat16)
    return key * flag, jnp.concatenate([value * flag, flag], axis=1)


def blocks_of(table, s, parts, skip=0):
    limit = table[s * PIECES]
    ks, vs = [], []
    for ref, at in parts:
        for i in range(skip, ref.shape[0]):
            key, value = kept(ref[i, 0], ref[i, 1], table[at + i] < limit)
            ks.append(key)
            vs.append(value)
    return ks, vs


def weigh(score, top, count):
    return jnp.exp2(score * SCALE2 - jnp.concatenate([top] * count, axis=1)).astype(jnp.bfloat16)


def tile_rows(tile):
    return slice(tile * TILE * SP, (tile + 1) * TILE * SP)


def leaving(sems, s, piece, *pairs):
    rows = (FRONT, BACK)[piece]
    return [
        pltpu.make_async_copy(ref.at[s, rows], out.at[s, rows], sems.at[2 * piece + k, s])
        for k, (ref, out) in enumerate(pairs)
    ]


def first_kernel(table, q_ref, a_ref, b_ref, top_out, acc_out, top_ref, acc, sems):
    def span(s, carry):
        swapped = jnp.full((2, SP, DH), s) > 0
        own = jnp.where(swapped, b_ref[0], a_ref[0])
        other = jnp.where(swapped, a_ref[0], b_ref[0])
        near_first = table[(1 - s) * PIECES] < table[s * PIECES]
        ks, vs = blocks_of(table, s, ((a_ref, 0), (b_ref, PIECES)), 1)
        key, value = kept(other[0], other[1], near_first)
        ones = jnp.ones((SP, DH), jnp.bfloat16)
        kg = jnp.concatenate([own[0], key] + ks, 0)
        vg = jnp.concatenate([jnp.concatenate([own[1], ones], axis=1), value] + vs, 0)
        for tile in range(HEADS // TILE):
            at = tile_rows(tile)
            score = lax.dot_general(
                queries_of(q_ref, s, tile), kg, NT, preferred_element_type=jnp.float32
            )
            row = lax.broadcasted_iota(jnp.int32, (TILE * SP, SP), 0) % SP
            keep = lax.broadcasted_iota(jnp.int32, (TILE * SP, SP), 1) <= row
            diagonal = jnp.where(keep, score[:, :SP] * SCALE2, -1e30)
            top = jnp.broadcast_to(jnp.max(diagonal, axis=1, keepdims=True), (TILE * SP, SP))
            top_ref[s, at, :] = top
            near = jnp.where(keep, jnp.exp2(diagonal - top), 0.0).astype(jnp.bfloat16)
            weight = jnp.concatenate([near, weigh(score[:, SP:], top, len(ks) + 1)], axis=1)
            acc[s, at, :] = jnp.dot(weight, vg, preferred_element_type=jnp.float32)
            if tile == HEADS // TILE - 2:
                for copy in leaving(sems, s, 0, (top_ref, top_out), (acc, acc_out)):
                    copy.start()
        for copy in leaving(sems, s, 1, (top_ref, top_out), (acc, acc_out)):
            copy.start()
        return carry

    lax.fori_loop(0, 2, span, 0)
    for s in range(2):
        for piece in range(2):
            for copy in leaving(sems, s, piece, (top_ref, top_out), (acc, acc_out)):
                copy.wait()


def span_sums(s, table, q_ref, parts, top_ref, store):
    ks, vs = blocks_of(table, s, parts)
    kg, vg = jnp.concatenate(ks, 0), jnp.concatenate(vs, 0)
    for tile in range(HEADS // TILE):
        score = lax.dot_general(
            queries_of(q_ref, s, tile), kg, NT, preferred_element_type=jnp.float32
        )
        weight = weigh(score, top_ref[s, tile_rows(tile), :], len(ks))
        store(tile, jnp.dot(weight, vg, preferred_element_type=jnp.float32))


def next_kernel(firsts, table, q_ref, top_in, acc_in, *refs):
    *pieces, acc_out, top_ref, acc, sems = refs
    parts = tuple(zip(pieces, firsts))
    ins = ((top_in, top_ref), (acc_in, acc))
    for k, (i, o) in enumerate(ins):
        pltpu.make_async_copy(i.at[0], o.at[0], sems.at[k, 0]).start()

    def span(s, carry):
        for k, (i, o) in enumerate(ins):
            pltpu.make_async_copy(i.at[s], o.at[s], sems.at[k, s]).wait()

        @pl.when(s == 0)
        def _():
            for k, (i, o) in enumerate(ins):
                pltpu.make_async_copy(i.at[1], o.at[1], sems.at[k, 1]).start()

        def store(tile, sums):
            at = tile_rows(tile)
            acc[s, at, :] = acc[s, at, :] + sums
            if tile == HEADS // TILE - 2:
                pltpu.make_async_copy(acc.at[s, FRONT], acc_out.at[s, FRONT], sems.at[2, s]).start()

        span_sums(s, table, q_ref, parts, top_ref, store)
        pltpu.make_async_copy(acc.at[s, BACK], acc_out.at[s, BACK], sems.at[3, s]).start()
        return carry

    lax.fori_loop(0, 2, span, 0)
    for s in range(2):
        pltpu.make_async_copy(acc.at[s, FRONT], acc_out.at[s, FRONT], sems.at[2, s]).wait()
        pltpu.make_async_copy(acc.at[s, BACK], acc_out.at[s, BACK], sems.at[3, s]).wait()


def last_kernel(
    table, q_ref, top_in, acc_in, b_ref, mine, core, zh, other, sa, sb, ra, rb,
    out, pages, scales,
    top_ref, acc, hold, sems, worst, far_v, far,
):
    ins = ((top_in, top_ref), (acc_in, acc))
    for s in range(2):
        for k, (i, o) in enumerate(ins):
            pltpu.make_async_copy(i.at[s], o.at[s], sems.at[k, s]).start()
    place(mine, core, zh, other, pages, scales)
    worst[...] = jnp.zeros_like(worst)

    def span(s, carry):
        for k, (i, o) in enumerate(ins):
            pltpu.make_async_copy(i.at[s], o.at[s], sems.at[k, s]).wait()

        def store(tile, sums):
            at = tile_rows(tile)
            both = acc[s, at, :] + sums
            total = both[:, DH:]
            worst[...] = jnp.where(total < LIMIT, worst[...], 1.0)
            done = (both[:, :DH] / total).astype(jnp.bfloat16)
            for h in range(TILE):
                head = tile * TILE + h
                rows = pl.ds(pl.multiple_of(s * SP, SP), SP)
                out[rows, head * DH : (head + 1) * DH] = done[h * SP : (h + 1) * SP]

        span_sums(s, table, q_ref, ((b_ref, PIECES + PIECES // 2),), top_ref, store)
        return carry

    lax.fori_loop(0, 2, span, 0)

    @pl.when(jnp.max(worst[...]) > 0.0)
    def _():
        half = PIECES // 2
        fetch = [
            pltpu.make_async_copy(ref, far_v.at[pl.ds(k * half, half)], far.at[k])
            for k, ref in enumerate((sa, ra, sb, rb))
        ]
        for copy in fetch:
            copy.start()
        for copy in fetch:
            copy.wait()
        rescaled(table, q_ref, far_v, out, acc.at[0], hold)


def rescaled(table, q_ref, held, out, acc, hold):
    for s in range(2):
        limit = table[s * PIECES]
        hold[...] = jnp.full_like(hold, -1e30)
        acc[...] = jnp.zeros_like(acc)

        def block(i, carry, s=s, limit=limit):
            pos = table[i]

            @pl.when(pos <= limit)
            def _():
                key = held[i, 0]
                value = held[i, 1]

                def head(h, c):
                    at = pl.ds(pl.multiple_of(h * SP, SP), SP)
                    q = q_ref[rows_of(s), pl.ds(pl.multiple_of(h * DH, DH), DH)]
                    score = lax.dot_general(q, key, NT, preferred_element_type=jnp.float32)
                    row = lax.broadcasted_iota(jnp.int32, (SP, SP), 0)
                    col = lax.broadcasted_iota(jnp.int32, (SP, SP), 1)
                    keep = (col + pos * SP) <= (row + limit * SP)
                    score = jnp.where(keep, score * SCALE2, -1e30)
                    old = hold[at, :]
                    new = jnp.maximum(old, jnp.max(score, axis=1, keepdims=True))
                    hold[at, :] = new
                    factor = jnp.exp2(old - new)
                    weight = jnp.where(keep, jnp.exp2(score - new), 0.0)
                    acc[at, :DH] = acc[at, :DH] * factor + jnp.dot(
                        weight.astype(jnp.bfloat16), value, preferred_element_type=jnp.float32
                    )
                    acc[at, DH:] = acc[at, DH:] * factor + jnp.sum(weight, axis=1, keepdims=True)
                    return c

                lax.fori_loop(0, HEADS, head, 0)

            return carry

        lax.fori_loop(0, 2 * PIECES, block, 0)
        for h in range(HEADS):
            out[rows_of(s), h * DH : (h + 1) * DH] = (
                acc[rows_of(h), :DH] / acc[rows_of(h), DH:]
            ).astype(jnp.bfloat16)


def pick_kernel(table, sa, ra, sb, rb, pages, sems):
    half = PIECES // 2
    for j in range(2):
        want = table[2 * PIECES + j]
        for k, ref in enumerate((sa, ra, sb, rb)):

            @pl.when((want >= k * half) & (want < (k + 1) * half))
            def _():
                at = jnp.clip(want - k * half, 0, half - 1)
                pltpu.make_async_copy(ref.at[at], pages.at[j], sems.at[j]).start()

    for j in range(2):
        pltpu.make_async_copy(sa.at[0], pages.at[j], sems.at[j]).wait()


def place(mine, core, zh, other, pages, scales):
    me = lax.axis_index("zh") * 2 + lax.axis_index("core")
    lane = lax.broadcasted_iota(jnp.int32, (1, 4), 1)
    for j in range(2):
        for kind in range(2):
            row = jnp.zeros((1, 4), jnp.float32)
            for away, ref in enumerate((mine, core, zh, other)):
                head = me ^ away
                raw = ref[j, kind].astype(jnp.float32)
                high = jnp.max(jnp.abs(raw), axis=0, keepdims=True)
                scale = jnp.max(high, axis=1, keepdims=True) + 1e-06
                row = jnp.where(lane == head, scale, row)
                pages[j, head, kind] = (raw / scale).astype(jnp.bfloat16)
            scales[j, kind : kind + 1, :] = row


def f32(*shape):
    return jax.ShapeDtypeStruct(shape, jnp.float32)


def bf16(*shape):
    return jax.ShapeDtypeStruct(shape, jnp.bfloat16)


def options(spans):
    return {
        "compiler_params": pltpu.CompilerParams(vmem_limit_bytes=56 * 2**20),
        "cost_estimate": pl.CostEstimate(
            flops=4 * 2 * ROWS * spans * SP * DH * 2,
            transcendentals=2 * ROWS * spans * SP,
            bytes_accessed=8 * 2**20,
        ),
    }


TOPS = (2, ROWS, DH)
SUMS = (2, ROWS, 2 * DH)


def state():
    return [
        pltpu.VMEM(TOPS, jnp.float32),
        pltpu.VMEM(SUMS, jnp.float32),
        pltpu.SemaphoreType.DMA((4, 2)),
    ]


def sums_of(firsts, name, table, queries, top, acc, *pieces):
    return pl.pallas_call(
        lambda *refs: next_kernel(firsts, *refs),
        out_shape=f32(*SUMS),
        in_specs=[SM, VM, ANY, ANY] + [VM] * len(pieces),
        out_specs=ANY,
        scratch_shapes=state(),
        name=name,
        **options(sum(p.shape[0] for p in pieces)),
    )(table, queries, top, acc, *pieces)


def swap(x, along_first, mask):
    pairs = []
    for y in range(4):
        for xx in range(4):
            for core in range(2):
                on_x = (core == 0) == along_first
                there = (y, xx ^ mask) if on_x else (y ^ mask, xx)
                pairs.append(((y * 4 + xx) * 2 + core, (there[0] * 4 + there[1]) * 2 + core))
    return lax.ppermute(x, ("y", "x", "core"), pairs)


def on_device(queries, keys, values, span_table, page_slots):
    own = jnp.stack([keys.reshape(2, SP, DH), values.reshape(2, SP, DH)], axis=1)[:, None]
    both = jnp.concatenate([own, lax.ppermute(own, "zl", [(0, 1), (1, 0)])], axis=1)
    table = tables(span_table, page_slots)
    held = [both[0], both[1]]

    def exchange(held, along_first, stage):
        return [swap(held[p], along_first, MASKS[p][stage]) for p in range(2)]

    def grown(held, come):
        return [jnp.concatenate([held[p], come[p]], axis=0) for p in range(2)]

    held = grown(held, exchange(held, True, 0))
    come = exchange(held, True, 1)
    top, acc = pl.pallas_call(
        first_kernel,
        out_shape=(f32(*TOPS), f32(*SUMS)),
        in_specs=[SM] + [VM] * 3,
        out_specs=(ANY, ANY),
        scratch_shapes=state(),
        name="attend_first",
        **options(8),
    )(table, queries, held[0], held[1])
    for stage in range(2):
        more = come
        held = grown(held, come)
        held[0], held[1], acc = lax.optimization_barrier((held[0], held[1], acc))
        come = exchange(held, False, stage)
        at = 4 << stage
        acc = sums_of(
            (at, PIECES + at), ("attend_second", "attend_third")[stage], table, queries, top, acc, *more
        )
    mine = pl.pallas_call(
        pick_kernel,
        out_shape=bf16(2, 2, SP, DH),
        in_specs=[SM] + [ANY] * 4,
        out_specs=VM,
        scratch_shapes=[pltpu.SemaphoreType.DMA((2,))],
        name="pick_pages",
    )(table, held[0], come[0], held[1], come[1])
    others = [
        lax.ppermute(mine, ("zh", "core"), [(i, i ^ away) for i in range(4)]) for away in (1, 2, 3)
    ]
    acc = sums_of((16,), "attend_fourth", table, queries, top, acc, come[0])
    attended, pages, scales = pl.pallas_call(
        last_kernel,
        out_shape=(bf16(2 * SP, HEADS * DH), bf16(2, 4, 2, SP, DH), f32(2, 2, 4)),
        in_specs=[SM, VM] + [ANY] * 2 + [VM] * 5 + [ANY] * 4,
        out_specs=(VM, VM, VM),
        scratch_shapes=[
            pltpu.VMEM(TOPS, jnp.float32),
            pltpu.VMEM(SUMS, jnp.float32),
            pltpu.VMEM((ROWS, DH), jnp.float32),
            pltpu.SemaphoreType.DMA((2, 2)),
            pltpu.VMEM((TILE * SP, DH), jnp.float32),
            pltpu.VMEM((2 * PIECES, 2, SP, DH), jnp.bfloat16),
            pltpu.SemaphoreType.DMA((4,)),
        ],
        name="attend_last",
        **options(16),
    )(
        table, queries, top, acc, come[1], mine, *others,
        held[0], held[1], come[0], come[1],
    )
    return attended, pages, scales.transpose(0, 2, 1)


def solution(mesh):
    fine = Mesh(mesh.devices.reshape(4, 2, 4, 2, 2), ("y", "zl", "x", "zh", "core"))
    ctx, page = ("y", "zl", "x"), ("zh", "core")
    return jax.shard_map(
        on_device,
        mesh=fine,
        in_specs=(P(ctx, page), P(ctx, page), P(ctx, page), P(), P()),
        out_specs=(P(ctx, page), P(ctx, None, None, None, None), P(ctx, None, None)),
        check_vma=False,
    )
```

```python
import jax
import jax.numpy as jnp
from jax import lax
from jax.experimental import pallas as pl
from jax.experimental.pallas import tpu as pltpu
from jax.sharding import Mesh, PartitionSpec as P

DH = 128
SP = 128
HEADS = 16
ROWS = HEADS * SP
SCALE2 = DH ** (-0.5) * 1.4426950408889634
TILE = 4
LIMIT = 2.0**100
FRONT = pl.ds(0, ROWS - TILE * SP)
BACK = pl.ds(ROWS - TILE * SP, TILE * SP)
NT = (((1,), (1,)), ((), ()))
MASKS = ((1, 3), (3, 1))
PIECES = 32
ANY = pl.BlockSpec(memory_space=pl.ANY)
VM = pl.BlockSpec(memory_space=pltpu.VMEM)
SM = pl.BlockSpec(memory_space=pltpu.SMEM)


def tables(span_table, page_slots):
    y, zl, x, core = (lax.axis_index(a) for a in ("y", "zl", "x", "core"))
    index = jnp.arange(2 * PIECES, dtype=jnp.int32)
    part, piece = index // PIECES, index % PIECES
    bit = lambda i: (piece >> i) & 1
    low, high = 1 + 2 * part, 3 - 2 * part
    first = (bit(1) * low) ^ (bit(2) * high)
    second = (bit(3) * low) ^ (bit(4) * high)
    dx = jnp.where(core == 0, first, second)
    dy = jnp.where(core == 0, second, first)
    span = ((y ^ dy) * 8 + (zl ^ bit(0)) * 4 + (x ^ dx)) * 2 + part
    here = span[:, None] == jnp.arange(2 * PIECES, dtype=jnp.int32)[None, :]
    pos = jnp.sum(jnp.where(here, span_table[None, :], 0), axis=1)
    slot = jnp.sum(jnp.where(here, page_slots[None, :], 0), axis=1)
    mine = (y * 8 + zl * 4 + x) * 2 + jnp.arange(2, dtype=jnp.int32)
    want = jnp.sum(jnp.where(slot[None, :] == mine[:, None], index[None, :], 0), axis=1)
    return jnp.concatenate([pos, want])


def rows_of(s):
    return pl.ds(s * SP, SP)


def queries_of(q_ref, s, tile):
    rows = pl.ds(pl.multiple_of(s * SP, SP), SP)
    return jnp.concatenate(
        [q_ref[rows, (tile * TILE + h) * DH : (tile * TILE + h + 1) * DH] for h in range(TILE)], 0
    )


def kept(key, value, keep):
    flag = jnp.full((SP, DH), keep.astype(jnp.float32)).astype(jnp.bfloat16)
    return key * flag, jnp.concatenate([value * flag, flag], axis=1)


def blocks_of(table, s, parts, skip=0):
    limit = table[s * PIECES]
    ks, vs = [], []
    for ref, at in parts:
        for i in range(skip, ref.shape[0]):
            key, value = kept(ref[i, 0], ref[i, 1], table[at + i] < limit)
            ks.append(key)
            vs.append(value)
    return ks, vs


def weigh(score, top, count):
    return jnp.exp2(score * SCALE2 - jnp.concatenate([top] * count, axis=1)).astype(jnp.bfloat16)


def tile_rows(tile):
    return slice(tile * TILE * SP, (tile + 1) * TILE * SP)


def leaving(sems, s, piece, *pairs):
    rows = (FRONT, BACK)[piece]
    return [
        pltpu.make_async_copy(ref.at[s, rows], out.at[s, rows], sems.at[2 * piece + k, s])
        for k, (ref, out) in enumerate(pairs)
    ]


def first_kernel(table, q_ref, a_ref, b_ref, top_out, acc_out, top_ref, acc, sems):
    def span(s, carry):
        swapped = jnp.full((2, SP, DH), s) > 0
        own = jnp.where(swapped, b_ref[0], a_ref[0])
        other = jnp.where(swapped, a_ref[0], b_ref[0])
        near_first = table[(1 - s) * PIECES] < table[s * PIECES]
        ks, vs = blocks_of(table, s, ((a_ref, 0), (b_ref, PIECES)), 1)
        key, value = kept(other[0], other[1], near_first)
        ones = jnp.ones((SP, DH), jnp.bfloat16)
        kg = jnp.concatenate([own[0], key] + ks, 0)
        vg = jnp.concatenate([jnp.concatenate([own[1], ones], axis=1), value] + vs, 0)
        for tile in range(HEADS // TILE):
            at = tile_rows(tile)
            score = lax.dot_general(
                queries_of(q_ref, s, tile), kg, NT, preferred_element_type=jnp.float32
            )
            row = lax.broadcasted_iota(jnp.int32, (TILE * SP, SP), 0) % SP
            keep = lax.broadcasted_iota(jnp.int32, (TILE * SP, SP), 1) <= row
            diagonal = jnp.where(keep, score[:, :SP] * SCALE2, -1e30)
            top = jnp.broadcast_to(jnp.max(diagonal, axis=1, keepdims=True), (TILE * SP, SP))
            top_ref[s, at, :] = top
            near = jnp.where(keep, jnp.exp2(diagonal - top), 0.0).astype(jnp.bfloat16)
            weight = jnp.concatenate([near, weigh(score[:, SP:], top, len(ks) + 1)], axis=1)
            acc[s, at, :] = jnp.dot(weight, vg, preferred_element_type=jnp.float32)
            if tile == HEADS // TILE - 2:
                for copy in leaving(sems, s, 0, (top_ref, top_out), (acc, acc_out)):
                    copy.start()
        for copy in leaving(sems, s, 1, (top_ref, top_out), (acc, acc_out)):
            copy.start()
        return carry

    lax.fori_loop(0, 2, span, 0)
    for s in range(2):
        for piece in range(2):
            for copy in leaving(sems, s, piece, (top_ref, top_out), (acc, acc_out)):
                copy.wait()


def span_sums(s, table, q_ref, parts, top_ref, store):
    ks, vs = blocks_of(table, s, parts)
    kg, vg = jnp.concatenate(ks, 0), jnp.concatenate(vs, 0)
    for tile in range(HEADS // TILE):
        score = lax.dot_general(
            queries_of(q_ref, s, tile), kg, NT, preferred_element_type=jnp.float32
        )
        weight = weigh(score, top_ref[s, tile_rows(tile), :], len(ks))
        store(tile, jnp.dot(weight, vg, preferred_element_type=jnp.float32))


def next_kernel(firsts, table, q_ref, top_in, acc_in, *refs):
    *pieces, acc_out, top_ref, acc, sems = refs
    parts = tuple(zip(pieces, firsts))
    ins = ((top_in, top_ref), (acc_in, acc))
    for k, (i, o) in enumerate(ins):
        pltpu.make_async_copy(i.at[0], o.at[0], sems.at[k, 0]).start()

    def span(s, carry):
        for k, (i, o) in enumerate(ins):
            pltpu.make_async_copy(i.at[s], o.at[s], sems.at[k, s]).wait()

        @pl.when(s == 0)
        def _():
            for k, (i, o) in enumerate(ins):
                pltpu.make_async_copy(i.at[1], o.at[1], sems.at[k, 1]).start()

        def store(tile, sums):
            at = tile_rows(tile)
            acc[s, at, :] = acc[s, at, :] + sums
            if tile == HEADS // TILE - 2:
                pltpu.make_async_copy(acc.at[s, FRONT], acc_out.at[s, FRONT], sems.at[2, s]).start()

        span_sums(s, table, q_ref, parts, top_ref, store)
        pltpu.make_async_copy(acc.at[s, BACK], acc_out.at[s, BACK], sems.at[3, s]).start()
        return carry

    lax.fori_loop(0, 2, span, 0)
    for s in range(2):
        pltpu.make_async_copy(acc.at[s, FRONT], acc_out.at[s, FRONT], sems.at[2, s]).wait()
        pltpu.make_async_copy(acc.at[s, BACK], acc_out.at[s, BACK], sems.at[3, s]).wait()


def last_kernel(
    table, q_ref, top_in, acc_in, a_ref, b_ref, sa, sb, ra, rb,
    out,
    top_ref, acc, hold, sems, worst, far_v, far,
):
    ins = ((top_in, top_ref), (acc_in, acc))
    for s in range(2):
        for k, (i, o) in enumerate(ins):
            pltpu.make_async_copy(i.at[s], o.at[s], sems.at[k, s]).start()
    worst[...] = jnp.zeros_like(worst)

    def span(s, carry):
        for k, (i, o) in enumerate(ins):
            pltpu.make_async_copy(i.at[s], o.at[s], sems.at[k, s]).wait()

        def store(tile, sums):
            at = tile_rows(tile)
            both = acc[s, at, :] + sums
            total = both[:, DH:]
            worst[...] = jnp.where(total < LIMIT, worst[...], 1.0)
            done = (both[:, :DH] / total).astype(jnp.bfloat16)
            for h in range(TILE):
                head = tile * TILE + h
                rows = pl.ds(pl.multiple_of(s * SP, SP), SP)
                out[rows, head * DH : (head + 1) * DH] = done[h * SP : (h + 1) * SP]

        parts = ((a_ref, PIECES // 2), (b_ref, PIECES + PIECES // 2))
        span_sums(s, table, q_ref, parts, top_ref, store)
        return carry

    lax.fori_loop(0, 2, span, 0)

    @pl.when(jnp.max(worst[...]) > 0.0)
    def _():
        half = PIECES // 2
        fetch = [
            pltpu.make_async_copy(ref, far_v.at[pl.ds(k * half, half)], far.at[k])
            for k, ref in enumerate((sa, ra, sb, rb))
        ]
        for copy in fetch:
            copy.start()
        for copy in fetch:
            copy.wait()
        rescaled(table, q_ref, far_v, out, acc.at[0], hold)


def rescaled(table, q_ref, held, out, acc, hold):
    for s in range(2):
        limit = table[s * PIECES]
        hold[...] = jnp.full_like(hold, -1e30)
        acc[...] = jnp.zeros_like(acc)

        def block(i, carry, s=s, limit=limit):
            pos = table[i]

            @pl.when(pos <= limit)
            def _():
                key = held[i, 0]
                value = held[i, 1]

                def head(h, c):
                    at = pl.ds(pl.multiple_of(h * SP, SP), SP)
                    q = q_ref[rows_of(s), pl.ds(pl.multiple_of(h * DH, DH), DH)]
                    score = lax.dot_general(q, key, NT, preferred_element_type=jnp.float32)
                    row = lax.broadcasted_iota(jnp.int32, (SP, SP), 0)
                    col = lax.broadcasted_iota(jnp.int32, (SP, SP), 1)
                    keep = (col + pos * SP) <= (row + limit * SP)
                    score = jnp.where(keep, score * SCALE2, -1e30)
                    old = hold[at, :]
                    new = jnp.maximum(old, jnp.max(score, axis=1, keepdims=True))
                    hold[at, :] = new
                    factor = jnp.exp2(old - new)
                    weight = jnp.where(keep, jnp.exp2(score - new), 0.0)
                    acc[at, :DH] = acc[at, :DH] * factor + jnp.dot(
                        weight.astype(jnp.bfloat16), value, preferred_element_type=jnp.float32
                    )
                    acc[at, DH:] = acc[at, DH:] * factor + jnp.sum(weight, axis=1, keepdims=True)
                    return c

                lax.fori_loop(0, HEADS, head, 0)

            return carry

        lax.fori_loop(0, 2 * PIECES, block, 0)
        for h in range(HEADS):
            out[rows_of(s), h * DH : (h + 1) * DH] = (
                acc[rows_of(h), :DH] / acc[rows_of(h), DH:]
            ).astype(jnp.bfloat16)


def pick_kernel(table, sa, ra, sb, rb, pages, sems):
    half = PIECES // 2
    for j in range(2):
        want = table[2 * PIECES + j]
        for k, ref in enumerate((sa, ra, sb, rb)):

            @pl.when((want >= k * half) & (want < (k + 1) * half))
            def _():
                at = jnp.clip(want - k * half, 0, half - 1)
                pltpu.make_async_copy(ref.at[at], pages.at[j], sems.at[j]).start()

    for j in range(2):
        pltpu.make_async_copy(sa.at[0], pages.at[j], sems.at[j]).wait()


def place(mine, core, zh, other, pages, scales):
    me = lax.axis_index("zh") * 2 + lax.axis_index("core")
    lane = lax.broadcasted_iota(jnp.int32, (1, 4), 1)
    for j in range(2):
        for kind in range(2):
            row = jnp.zeros((1, 4), jnp.float32)
            for away, ref in enumerate((mine, core, zh, other)):
                head = me ^ away
                raw = ref[j, kind].astype(jnp.float32)
                high = jnp.max(jnp.abs(raw), axis=0, keepdims=True)
                scale = jnp.max(high, axis=1, keepdims=True) + 1e-06
                row = jnp.where(lane == head, scale, row)
                pages[j, head, kind] = (raw / scale).astype(jnp.bfloat16)
            scales[j, kind : kind + 1, :] = row


def f32(*shape):
    return jax.ShapeDtypeStruct(shape, jnp.float32)


def bf16(*shape):
    return jax.ShapeDtypeStruct(shape, jnp.bfloat16)


def options(spans):
    return {
        "compiler_params": pltpu.CompilerParams(vmem_limit_bytes=56 * 2**20),
        "cost_estimate": pl.CostEstimate(
            flops=4 * 2 * ROWS * spans * SP * DH * 2,
            transcendentals=2 * ROWS * spans * SP,
            bytes_accessed=8 * 2**20,
        ),
    }


TOPS = (2, ROWS, DH)
SUMS = (2, ROWS, 2 * DH)


def state():
    return [
        pltpu.VMEM(TOPS, jnp.float32),
        pltpu.VMEM(SUMS, jnp.float32),
        pltpu.SemaphoreType.DMA((4, 2)),
    ]


def sums_of(firsts, name, table, queries, top, acc, *pieces):
    return pl.pallas_call(
        lambda *refs: next_kernel(firsts, *refs),
        out_shape=f32(*SUMS),
        in_specs=[SM, VM, ANY, ANY] + [VM] * len(pieces),
        out_specs=ANY,
        scratch_shapes=state(),
        name=name,
        **options(sum(p.shape[0] for p in pieces)),
    )(table, queries, top, acc, *pieces)


def swap(x, along_first, mask):
    pairs = []
    for y in range(4):
        for xx in range(4):
            for core in range(2):
                on_x = (core == 0) == along_first
                there = (y, xx ^ mask) if on_x else (y ^ mask, xx)
                pairs.append(((y * 4 + xx) * 2 + core, (there[0] * 4 + there[1]) * 2 + core))
    return lax.ppermute(x, ("y", "x", "core"), pairs)


def on_device(queries, keys, values, span_table, page_slots):
    own = jnp.stack([keys.reshape(2, SP, DH), values.reshape(2, SP, DH)], axis=1)[:, None]
    both = jnp.concatenate([own, lax.ppermute(own, "zl", [(0, 1), (1, 0)])], axis=1)
    table = tables(span_table, page_slots)
    held = [both[0], both[1]]

    def exchange(held, along_first, stage):
        return [swap(held[p], along_first, MASKS[p][stage]) for p in range(2)]

    def grown(held, come):
        return [jnp.concatenate([held[p], come[p]], axis=0) for p in range(2)]

    held = grown(held, exchange(held, True, 0))
    come = exchange(held, True, 1)
    top, acc = pl.pallas_call(
        first_kernel,
        out_shape=(f32(*TOPS), f32(*SUMS)),
        in_specs=[SM] + [VM] * 3,
        out_specs=(ANY, ANY),
        scratch_shapes=state(),
        name="attend_first",
        **options(8),
    )(table, queries, held[0], held[1])
    for stage in range(2):
        more = come
        held = grown(held, come)
        held[0], held[1], acc = lax.optimization_barrier((held[0], held[1], acc))
        come = exchange(held, False, stage)
        at = 4 << stage
        acc = sums_of(
            (at, PIECES + at), ("attend_second", "attend_third")[stage], table, queries, top, acc, *more
        )
    mine = pl.pallas_call(
        pick_kernel,
        out_shape=bf16(2, 2, SP, DH),
        in_specs=[SM] + [ANY] * 4,
        out_specs=VM,
        scratch_shapes=[pltpu.SemaphoreType.DMA((2,))],
        name="pick_pages",
    )(table, held[0], come[0], held[1], come[1])
    others = [
        lax.ppermute(mine, ("zh", "core"), [(i, i ^ away) for i in range(4)]) for away in (1, 2, 3)
    ]
    attended = pl.pallas_call(
        last_kernel,
        out_shape=bf16(2 * SP, HEADS * DH),
        in_specs=[SM, VM] + [ANY] * 2 + [VM] * 2 + [ANY] * 4,
        out_specs=VM,
        scratch_shapes=[
            pltpu.VMEM(TOPS, jnp.float32),
            pltpu.VMEM(SUMS, jnp.float32),
            pltpu.VMEM((ROWS, DH), jnp.float32),
            pltpu.SemaphoreType.DMA((2, 2)),
            pltpu.VMEM((TILE * SP, DH), jnp.float32),
            pltpu.VMEM((2 * PIECES, 2, SP, DH), jnp.bfloat16),
            pltpu.SemaphoreType.DMA((4,)),
        ],
        name="attend_last",
        **options(32),
    )(table, queries, top, acc, come[0], come[1], held[0], held[1], come[0], come[1])
    pages, scales = pl.pallas_call(
        place,
        out_shape=(bf16(2, 4, 2, SP, DH), f32(2, 2, 4)),
        in_specs=[VM] * 4,
        out_specs=(VM, VM),
        name="place_pages",
    )(mine, *others)
    return attended, pages, scales.transpose(0, 2, 1)


def solution(mesh):
    fine = Mesh(mesh.devices.reshape(4, 2, 4, 2, 2), ("y", "zl", "x", "zh", "core"))
    ctx, page = ("y", "zl", "x"), ("zh", "core")
    return jax.shard_map(
        on_device,
        mesh=fine,
        in_specs=(P(ctx, page), P(ctx, page), P(ctx, page), P(), P()),
        out_specs=(P(ctx, page), P(ctx, None, None, None, None), P(ctx, None, None)),
        check_vma=False,
    )
```

```python
import jax
import jax.numpy as jnp
from jax import lax
from jax.experimental import pallas as pl
from jax.experimental.pallas import tpu as pltpu
from jax.sharding import Mesh, PartitionSpec as P

DH = 128
SP = 128
HEADS = 16
ROWS = HEADS * SP
SCALE2 = DH ** (-0.5) * 1.4426950408889634
TILE = 4
LIMIT = 2.0**100
FRONT = pl.ds(0, ROWS - TILE * SP)
BACK = pl.ds(ROWS - TILE * SP, TILE * SP)
NT = (((1,), (1,)), ((), ()))
MASKS = ((1, 3), (3, 1))
PIECES = 32
ANY = pl.BlockSpec(memory_space=pl.ANY)
VM = pl.BlockSpec(memory_space=pltpu.VMEM)
SM = pl.BlockSpec(memory_space=pltpu.SMEM)


def tables(span_table, page_slots):
    y, zl, x, core = (lax.axis_index(a) for a in ("y", "zl", "x", "core"))
    index = jnp.arange(2 * PIECES, dtype=jnp.int32)
    part, piece = index // PIECES, index % PIECES
    bit = lambda i: (piece >> i) & 1
    low, high = 1 + 2 * part, 3 - 2 * part
    first = (bit(1) * low) ^ (bit(2) * high)
    second = (bit(3) * low) ^ (bit(4) * high)
    dx = jnp.where(core == 0, first, second)
    dy = jnp.where(core == 0, second, first)
    span = ((y ^ dy) * 8 + (zl ^ bit(0)) * 4 + (x ^ dx)) * 2 + part
    here = span[:, None] == jnp.arange(2 * PIECES, dtype=jnp.int32)[None, :]
    pos = jnp.sum(jnp.where(here, span_table[None, :], 0), axis=1)
    slot = jnp.sum(jnp.where(here, page_slots[None, :], 0), axis=1)
    mine = (y * 8 + zl * 4 + x) * 2 + jnp.arange(2, dtype=jnp.int32)
    want = jnp.sum(jnp.where(slot[None, :] == mine[:, None], index[None, :], 0), axis=1)
    return jnp.concatenate([pos, want])


def rows_of(s):
    return pl.ds(s * SP, SP)


def queries_of(q_ref, s, tile):
    rows = pl.ds(pl.multiple_of(s * SP, SP), SP)
    return jnp.concatenate(
        [q_ref[rows, (tile * TILE + h) * DH : (tile * TILE + h + 1) * DH] for h in range(TILE)], 0
    )


def kept(key, value, keep):
    flag = jnp.full((SP, DH), keep.astype(jnp.float32)).astype(jnp.bfloat16)
    return key * flag, jnp.concatenate([value * flag, flag], axis=1)


def blocks_of(table, s, parts, skip=0):
    limit = table[s * PIECES]
    ks, vs = [], []
    for ref, at in parts:
        for i in range(skip, ref.shape[0]):
            key, value = kept(ref[i, 0], ref[i, 1], table[at + i] < limit)
            ks.append(key)
            vs.append(value)
    return ks, vs


def weigh(score, top, count):
    return jnp.exp2(score * SCALE2 - jnp.concatenate([top] * count, axis=1)).astype(jnp.bfloat16)


def tile_rows(tile):
    return slice(tile * TILE * SP, (tile + 1) * TILE * SP)


def leaving(sems, s, piece, *pairs):
    rows = (FRONT, BACK)[piece]
    return [
        pltpu.make_async_copy(ref.at[s, rows], out.at[s, rows], sems.at[2 * piece + k, s])
        for k, (ref, out) in enumerate(pairs)
    ]


def first_kernel(table, q_ref, a_ref, b_ref, top_out, acc_out, top_ref, acc, sems):
    def span(s, carry):
        swapped = jnp.full((2, SP, DH), s) > 0
        own = jnp.where(swapped, b_ref[0], a_ref[0])
        other = jnp.where(swapped, a_ref[0], b_ref[0])
        near_first = table[(1 - s) * PIECES] < table[s * PIECES]
        ks, vs = blocks_of(table, s, ((a_ref, 0), (b_ref, PIECES)), 1)
        key, value = kept(other[0], other[1], near_first)
        ones = jnp.ones((SP, DH), jnp.bfloat16)
        kg = jnp.concatenate([own[0], key] + ks, 0)
        vg = jnp.concatenate([jnp.concatenate([own[1], ones], axis=1), value] + vs, 0)
        for tile in range(HEADS // TILE):
            at = tile_rows(tile)
            score = lax.dot_general(
                queries_of(q_ref, s, tile), kg, NT, preferred_element_type=jnp.float32
            )
            row = lax.broadcasted_iota(jnp.int32, (TILE * SP, SP), 0) % SP
            keep = lax.broadcasted_iota(jnp.int32, (TILE * SP, SP), 1) <= row
            diagonal = jnp.where(keep, score[:, :SP] * SCALE2, -1e30)
            top = jnp.broadcast_to(jnp.max(diagonal, axis=1, keepdims=True), (TILE * SP, SP))
            top_ref[s, at, :] = top
            near = jnp.where(keep, jnp.exp2(diagonal - top), 0.0).astype(jnp.bfloat16)
            weight = jnp.concatenate([near, weigh(score[:, SP:], top, len(ks) + 1)], axis=1)
            acc[s, at, :] = jnp.dot(weight, vg, preferred_element_type=jnp.float32)
            if tile == HEADS // TILE - 2:
                for copy in leaving(sems, s, 0, (top_ref, top_out), (acc, acc_out)):
                    copy.start()
        for copy in leaving(sems, s, 1, (top_ref, top_out), (acc, acc_out)):
            copy.start()
        return carry

    lax.fori_loop(0, 2, span, 0)
    for s in range(2):
        for piece in range(2):
            for copy in leaving(sems, s, piece, (top_ref, top_out), (acc, acc_out)):
                copy.wait()


def span_sums(s, table, q_ref, parts, top_ref, store):
    ks, vs = blocks_of(table, s, parts)
    kg, vg = jnp.concatenate(ks, 0), jnp.concatenate(vs, 0)
    for tile in range(HEADS // TILE):
        score = lax.dot_general(
            queries_of(q_ref, s, tile), kg, NT, preferred_element_type=jnp.float32
        )
        weight = weigh(score, top_ref[s, tile_rows(tile), :], len(ks))
        store(tile, jnp.dot(weight, vg, preferred_element_type=jnp.float32))


def next_kernel(firsts, table, q_ref, top_in, acc_in, *refs):
    *pieces, acc_out, top_ref, acc, sems = refs
    parts = tuple(zip(pieces, firsts))
    ins = ((top_in, top_ref), (acc_in, acc))
    for k, (i, o) in enumerate(ins):
        pltpu.make_async_copy(i.at[0], o.at[0], sems.at[k, 0]).start()

    def span(s, carry):
        for k, (i, o) in enumerate(ins):
            pltpu.make_async_copy(i.at[s], o.at[s], sems.at[k, s]).wait()

        @pl.when(s == 0)
        def _():
            for k, (i, o) in enumerate(ins):
                pltpu.make_async_copy(i.at[1], o.at[1], sems.at[k, 1]).start()

        def store(tile, sums):
            at = tile_rows(tile)
            acc[s, at, :] = acc[s, at, :] + sums
            if tile == HEADS // TILE - 2:
                pltpu.make_async_copy(acc.at[s, FRONT], acc_out.at[s, FRONT], sems.at[2, s]).start()

        span_sums(s, table, q_ref, parts, top_ref, store)
        pltpu.make_async_copy(acc.at[s, BACK], acc_out.at[s, BACK], sems.at[3, s]).start()
        return carry

    lax.fori_loop(0, 2, span, 0)
    for s in range(2):
        pltpu.make_async_copy(acc.at[s, FRONT], acc_out.at[s, FRONT], sems.at[2, s]).wait()
        pltpu.make_async_copy(acc.at[s, BACK], acc_out.at[s, BACK], sems.at[3, s]).wait()


def last_kernel(
    table, q_ref, top_in, acc_in, a_ref, b_ref, sa, sb, ra, rb,
    result,
    top_ref, acc, hold, sems, worst, far_v, far, out, leave,
):
    ins = ((top_in, top_ref), (acc_in, acc))
    for s in range(2):
        for k, (i, o) in enumerate(ins):
            pltpu.make_async_copy(i.at[s], o.at[s], sems.at[k, s]).start()
    worst[...] = jnp.zeros_like(worst)

    def span(s, carry):
        for k, (i, o) in enumerate(ins):
            pltpu.make_async_copy(i.at[s], o.at[s], sems.at[k, s]).wait()

        def store(tile, sums):
            at = tile_rows(tile)
            both = acc[s, at, :] + sums
            total = both[:, DH:]
            worst[...] = jnp.where(total < LIMIT, worst[...], 1.0)
            done = (both[:, :DH] / total).astype(jnp.bfloat16)
            for h in range(TILE):
                head = tile * TILE + h
                rows = pl.ds(pl.multiple_of(s * SP, SP), SP)
                out[rows, head * DH : (head + 1) * DH] = done[h * SP : (h + 1) * SP]

        parts = ((a_ref, PIECES // 2), (b_ref, PIECES + PIECES // 2))
        span_sums(s, table, q_ref, parts, top_ref, store)
        mine = pl.ds(pl.multiple_of(s * SP, SP), SP)
        pltpu.make_async_copy(out.at[mine], result.at[mine], leave.at[s]).start()
        return carry

    lax.fori_loop(0, 2, span, 0)
    for s in range(2):
        mine = pl.ds(s * SP, SP)
        pltpu.make_async_copy(out.at[mine], result.at[mine], leave.at[s]).wait()

    @pl.when(jnp.max(worst[...]) > 0.0)
    def _():
        half = PIECES // 2
        fetch = [
            pltpu.make_async_copy(ref, far_v.at[pl.ds(k * half, half)], far.at[k])
            for k, ref in enumerate((sa, ra, sb, rb))
        ]
        for copy in fetch:
            copy.start()
        for copy in fetch:
            copy.wait()
        rescaled(table, q_ref, far_v, out, acc.at[0], hold)
        again = pltpu.make_async_copy(out, result, leave.at[0])
        again.start()
        again.wait()


def rescaled(table, q_ref, held, out, acc, hold):
    for s in range(2):
        limit = table[s * PIECES]
        hold[...] = jnp.full_like(hold, -1e30)
        acc[...] = jnp.zeros_like(acc)

        def block(i, carry, s=s, limit=limit):
            pos = table[i]

            @pl.when(pos <= limit)
            def _():
                key = held[i, 0]
                value = held[i, 1]

                def head(h, c):
                    at = pl.ds(pl.multiple_of(h * SP, SP), SP)
                    q = q_ref[rows_of(s), pl.ds(pl.multiple_of(h * DH, DH), DH)]
                    score = lax.dot_general(q, key, NT, preferred_element_type=jnp.float32)
                    row = lax.broadcasted_iota(jnp.int32, (SP, SP), 0)
                    col = lax.broadcasted_iota(jnp.int32, (SP, SP), 1)
                    keep = (col + pos * SP) <= (row + limit * SP)
                    score = jnp.where(keep, score * SCALE2, -1e30)
                    old = hold[at, :]
                    new = jnp.maximum(old, jnp.max(score, axis=1, keepdims=True))
                    hold[at, :] = new
                    factor = jnp.exp2(old - new)
                    weight = jnp.where(keep, jnp.exp2(score - new), 0.0)
                    acc[at, :DH] = acc[at, :DH] * factor + jnp.dot(
                        weight.astype(jnp.bfloat16), value, preferred_element_type=jnp.float32
                    )
                    acc[at, DH:] = acc[at, DH:] * factor + jnp.sum(weight, axis=1, keepdims=True)
                    return c

                lax.fori_loop(0, HEADS, head, 0)

            return carry

        lax.fori_loop(0, 2 * PIECES, block, 0)
        for h in range(HEADS):
            out[rows_of(s), h * DH : (h + 1) * DH] = (
                acc[rows_of(h), :DH] / acc[rows_of(h), DH:]
            ).astype(jnp.bfloat16)


def pick_kernel(table, sa, ra, sb, rb, pages, sems):
    half = PIECES // 2
    for j in range(2):
        want = table[2 * PIECES + j]
        for k, ref in enumerate((sa, ra, sb, rb)):

            @pl.when((want >= k * half) & (want < (k + 1) * half))
            def _():
                at = jnp.clip(want - k * half, 0, half - 1)
                pltpu.make_async_copy(ref.at[at], pages.at[j], sems.at[j]).start()

    for j in range(2):
        pltpu.make_async_copy(sa.at[0], pages.at[j], sems.at[j]).wait()


def place(mine, core, zh, other, pages, scales):
    me = lax.axis_index("zh") * 2 + lax.axis_index("core")
    lane = lax.broadcasted_iota(jnp.int32, (1, 4), 1)
    for j in range(2):
        for kind in range(2):
            row = jnp.zeros((1, 4), jnp.float32)
            for away, ref in enumerate((mine, core, zh, other)):
                head = me ^ away
                raw = ref[j, kind].astype(jnp.float32)
                high = jnp.max(jnp.abs(raw), axis=0, keepdims=True)
                scale = jnp.max(high, axis=1, keepdims=True) + 1e-06
                row = jnp.where(lane == head, scale, row)
                pages[j, head, kind] = (raw / scale).astype(jnp.bfloat16)
            scales[j, kind : kind + 1, :] = row


def f32(*shape):
    return jax.ShapeDtypeStruct(shape, jnp.float32)


def bf16(*shape):
    return jax.ShapeDtypeStruct(shape, jnp.bfloat16)


def options(spans):
    return {
        "compiler_params": pltpu.CompilerParams(vmem_limit_bytes=56 * 2**20),
        "cost_estimate": pl.CostEstimate(
            flops=4 * 2 * ROWS * spans * SP * DH * 2,
            transcendentals=2 * ROWS * spans * SP,
            bytes_accessed=8 * 2**20,
        ),
    }


TOPS = (2, ROWS, DH)
SUMS = (2, ROWS, 2 * DH)


def state():
    return [
        pltpu.VMEM(TOPS, jnp.float32),
        pltpu.VMEM(SUMS, jnp.float32),
        pltpu.SemaphoreType.DMA((4, 2)),
    ]


def sums_of(firsts, name, table, queries, top, acc, *pieces):
    return pl.pallas_call(
        lambda *refs: next_kernel(firsts, *refs),
        out_shape=f32(*SUMS),
        in_specs=[SM, VM, ANY, ANY] + [VM] * len(pieces),
        out_specs=ANY,
        scratch_shapes=state(),
        name=name,
        **options(sum(p.shape[0] for p in pieces)),
    )(table, queries, top, acc, *pieces)


def swap(x, along_first, mask):
    pairs = []
    for y in range(4):
        for xx in range(4):
            for core in range(2):
                on_x = (core == 0) == along_first
                there = (y, xx ^ mask) if on_x else (y ^ mask, xx)
                pairs.append(((y * 4 + xx) * 2 + core, (there[0] * 4 + there[1]) * 2 + core))
    return lax.ppermute(x, ("y", "x", "core"), pairs)


def on_device(queries, keys, values, span_table, page_slots):
    own = jnp.stack([keys.reshape(2, SP, DH), values.reshape(2, SP, DH)], axis=1)[:, None]
    both = jnp.concatenate([own, lax.ppermute(own, "zl", [(0, 1), (1, 0)])], axis=1)
    table = tables(span_table, page_slots)
    held = [both[0], both[1]]

    def exchange(held, along_first, stage):
        return [swap(held[p], along_first, MASKS[p][stage]) for p in range(2)]

    def grown(held, come):
        return [jnp.concatenate([held[p], come[p]], axis=0) for p in range(2)]

    held = grown(held, exchange(held, True, 0))
    come = exchange(held, True, 1)
    top, acc = pl.pallas_call(
        first_kernel,
        out_shape=(f32(*TOPS), f32(*SUMS)),
        in_specs=[SM] + [VM] * 3,
        out_specs=(ANY, ANY),
        scratch_shapes=state(),
        name="attend_first",
        **options(8),
    )(table, queries, held[0], held[1])
    for stage in range(2):
        more = come
        held = grown(held, come)
        held[0], held[1], acc = lax.optimization_barrier((held[0], held[1], acc))
        come = exchange(held, False, stage)
        at = 4 << stage
        acc = sums_of(
            (at, PIECES + at), ("attend_second", "attend_third")[stage], table, queries, top, acc, *more
        )
    mine = pl.pallas_call(
        pick_kernel,
        out_shape=bf16(2, 2, SP, DH),
        in_specs=[SM] + [ANY] * 4,
        out_specs=VM,
        scratch_shapes=[pltpu.SemaphoreType.DMA((2,))],
        name="pick_pages",
    )(table, held[0], come[0], held[1], come[1])
    others = [
        lax.ppermute(mine, ("zh", "core"), [(i, i ^ away) for i in range(4)]) for away in (1, 2, 3)
    ]
    attended = pl.pallas_call(
        last_kernel,
        out_shape=bf16(2 * SP, HEADS * DH),
        in_specs=[SM, VM] + [ANY] * 2 + [VM] * 2 + [ANY] * 4,
        out_specs=ANY,
        scratch_shapes=[
            pltpu.VMEM(TOPS, jnp.float32),
            pltpu.VMEM(SUMS, jnp.float32),
            pltpu.VMEM((ROWS, DH), jnp.float32),
            pltpu.SemaphoreType.DMA((2, 2)),
            pltpu.VMEM((TILE * SP, DH), jnp.float32),
            pltpu.VMEM((2 * PIECES, 2, SP, DH), jnp.bfloat16),
            pltpu.SemaphoreType.DMA((4,)),
            pltpu.VMEM((2 * SP, HEADS * DH), jnp.bfloat16),
            pltpu.SemaphoreType.DMA((2,)),
        ],
        name="attend_last",
        **options(32),
    )(table, queries, top, acc, come[0], come[1], held[0], held[1], come[0], come[1])
    pages, scales = pl.pallas_call(
        place,
        out_shape=(bf16(2, 4, 2, SP, DH), f32(2, 2, 4)),
        in_specs=[VM] * 4,
        out_specs=(VM, VM),
        name="place_pages",
    )(mine, *others)
    return attended, pages, scales.transpose(0, 2, 1)


def solution(mesh):
    fine = Mesh(mesh.devices.reshape(4, 2, 4, 2, 2), ("y", "zl", "x", "zh", "core"))
    ctx, page = ("y", "zl", "x"), ("zh", "core")
    return jax.shard_map(
        on_device,
        mesh=fine,
        in_specs=(P(ctx, page), P(ctx, page), P(ctx, page), P(), P()),
        out_specs=(P(ctx, page), P(ctx, None, None, None, None), P(ctx, None, None)),
        check_vma=False,
    )
```
